256 devices in a mesh: patch: 128 (over x, z, y), strip: 2 (over core).
Axes of the slice: x: 4, y: 4, z: 8, core: 2. Of those that a mesh axis runs over, the one named last changes fastest.
Arguments:
- features: float32 [262144, 128], P(('patch', 'strip')), may hold values from -6 to 6
- lap_tiles: float32 [4096, 6, 4096], P(('patch', 'strip')), may hold values from -0.3125 to 0.3125
- columns: int32 [4096, 6], P(('patch', 'strip')), may hold values from 0 to 4095, as said below
- weights: float32 [3, 64, 64], replicated, may hold values from -0.75 to 0.75
- bias_term: float32 [64], replicated, may hold values from -4 to 4
- cotangent: float32 [262144, 128], P(('patch', 'strip')), may hold values from -6 to 6
Outputs:
- output: float32 [262144, 128], P(('patch', 'strip'))
- input_grad: float32 [262144, 128], P(('patch', 'strip'))
- weight_grad: float32 [3, 64, 64], replicated
- bias_grad: float32 [64], replicated
The draws below stay inside these ranges and needn't reach their ends.
Inputs may be any that keep to these rules, and one draw needn't show every extreme that they name: `columns`: entry 0 of a block's 6 entries is the block itself and entry 1 lies exactly 4 blocks before or after it; all entries of a block are distinct blocks within 4 of it in the cyclic order of the 4096 blocks.
All inputs are finite; a program needn't handle non-finite values.
Results may differ from the reference program's by a relative error of at most 0.0001.
Values sent between devices are 32-bit elements; how exact they have to be, the bound alone decides.
No kernel may reach another device: no remote copies, remote signals or barrier semaphores. Data moves between devices by JAX's collectives and lax.ppermute only.
A program may use at most 64 MiB of HBM per device.

```python
import math
import jax
import jax.numpy as jnp
from jax import lax

C = 64
BATCH = 2
PB = 64
NB = 6
HB = 4
BLK_DEV = 16
BLOCKS = 4096
PIXELS = 262144


def draw_columns(key, part):
    block_ids = jnp.arange(BLOCKS, dtype=jnp.int32)
    sign_key = jax.random.fold_in(key, 11)
    rank_key = jax.random.fold_in(key, 12)
    sign_pick = jax.random.randint(sign_key, (BLOCKS,), 0, 2).astype(jnp.int32) * 2 - 1
    far_offset = sign_pick * HB
    candidates = jnp.concatenate([jnp.arange(-HB, 0), jnp.arange(1, HB + 1)]).astype(jnp.int32)
    scores = jax.random.randint(rank_key, (BLOCKS, 2 * HB), 0, 1 << 20).astype(jnp.int32) * (2 * HB) + jnp.arange(2 * HB, dtype=jnp.int32)
    scores = jnp.where(candidates[None, :] == far_offset[:, None], -1, scores)
    ranking = jnp.argsort(scores, axis=1)
    chosen = jnp.take_along_axis(jnp.broadcast_to(candidates, (BLOCKS, 2 * HB)), ranking, axis=1)[:, :NB - 1]
    offsets = jnp.concatenate([jnp.zeros((BLOCKS, 1), jnp.int32), chosen], axis=1)
    return jnp.mod(block_ids[:, None] + offsets, BLOCKS).astype(jnp.int32)


def shard_levels(rng, dims, cuts, least, high):
    loudness, own = 1.0, jax.random.fold_in(rng, 6)
    for axis_at, shards_of in cuts:
        heights = jnp.exp(jax.random.uniform(jax.random.fold_in(own, axis_at), (shards_of,), jnp.float32, least / len(cuts), high / len(cuts)))
        loudness = loudness * jnp.repeat(heights, dims[axis_at] // shards_of).reshape([-1 if axis == axis_at else 1 for axis in range(len(dims))])
    return loudness


def centred(rng, dims, width, limit, cuts=(), held_as=jnp.bfloat16):
    drawn = jax.random.normal(rng, dims, jnp.float32) * width
    if len(cuts) > 0:
        drawn = shard_levels(rng, dims, cuts, -0.22, 0.18) * drawn
    return jnp.clip(drawn, min=-limit, max=limit).astype(held_as)


def setup_inputs(seed: int = 0) -> dict:
    key_of = jax.random.split(jax.random.key(seed), 7)
    return {
        "features": centred(key_of[0], (PIXELS, BATCH * C), 1.0, 6.0, ((0, 256),), jnp.float32),
        "lap_tiles": centred(key_of[1], (BLOCKS, NB, PB * PB), (NB * PB) ** -0.5, 0.3125, ((0, 256),), jnp.float32),
        "columns": draw_columns(jax.random.fold_in(key_of[6], 71), 0),
        "weights": centred(key_of[3], (3, C, C), C ** -0.5, 0.75, (), jnp.float32),
        "bias_term": centred(key_of[4], (C,), 1.0, 4.0, (), jnp.float32),
        "cotangent": centred(key_of[5], (PIXELS, BATCH * C), 1.0, 6.0, ((0, 256),), jnp.float32),
    }


highest = lax.Precision.HIGHEST

def apply_lap(blocks, lap_tiles, columns):
    groups = blocks.shape[0] // BLK_DEV
    tile_groups = lap_tiles.reshape(groups, BLK_DEV, NB, PB, PB)
    column_groups = columns.reshape(groups, BLK_DEV, NB)

    def one_group(pieces):
        tile_part, column_part = pieces
        picked = blocks[column_part]
        return jnp.einsum('bjpq,bjqf->bpf', tile_part, picked, precision=highest)
    return lax.map(one_group, (tile_groups, column_groups)).reshape(blocks.shape)

def apply_lap_t(blocks, lap_tiles, columns):
    groups = blocks.shape[0] // BLK_DEV
    feat_width = blocks.shape[2]
    tile_groups = lap_tiles.reshape(groups, BLK_DEV, NB, PB, PB)
    column_groups = columns.reshape(groups, BLK_DEV, NB)
    vector_groups = blocks.reshape(groups, BLK_DEV, PB, feat_width)

    def one_group(total, pieces):
        tile_part, column_part, vector_part = pieces
        contrib = jnp.einsum('bjpq,bpf->bjqf', tile_part, vector_part, precision=highest)
        total = total.at[column_part.reshape(-1)].add(contrib.reshape(-1, PB, feat_width))
        return (total, None)
    total, unused = lax.scan(one_group, jnp.zeros_like(blocks), (tile_groups, column_groups, vector_groups))
    return total

def reference(features, lap_tiles, columns, weights, bias_term, cotangent):
    pixel_count, feat_width = features.shape
    block_count = pixel_count // PB
    zeroth = features.reshape(block_count, PB, feat_width)
    first_term = apply_lap(zeroth, lap_tiles, columns)
    second_term = 2.0 * apply_lap(first_term, lap_tiles, columns) - zeroth
    cheb_terms = (zeroth, first_term, second_term)
    mixed_sum = jnp.einsum('nbc,cd->nbd', zeroth.reshape(pixel_count, BATCH, C), weights[0], precision=highest)
    mixed_sum = mixed_sum + jnp.einsum('nbc,cd->nbd', first_term.reshape(pixel_count, BATCH, C), weights[1], precision=highest)
    mixed_sum = mixed_sum + jnp.einsum('nbc,cd->nbd', second_term.reshape(pixel_count, BATCH, C), weights[2], precision=highest)
    output = (mixed_sum + bias_term).reshape(pixel_count, feat_width)
    grad_maps = cotangent.reshape(pixel_count, BATCH, C)
    back_zero = jnp.einsum('nbd,cd->nbc', grad_maps, weights[0], precision=highest).reshape(block_count, PB, feat_width)
    back_one = jnp.einsum('nbd,cd->nbc', grad_maps, weights[1], precision=highest).reshape(block_count, PB, feat_width)
    back_two = jnp.einsum('nbd,cd->nbc', grad_maps, weights[2], precision=highest).reshape(block_count, PB, feat_width)
    inner_sum = back_one + 2.0 * apply_lap_t(back_two, lap_tiles, columns)
    input_grad = (back_zero - back_two + apply_lap_t(inner_sum, lap_tiles, columns)).reshape(pixel_count, feat_width)
    grad_scale = 1.0 / math.sqrt(BATCH * pixel_count)
    weight_grad = jnp.stack([jnp.einsum('nbc,nbd->cd', term_part.reshape(pixel_count, BATCH, C), grad_maps, precision=highest) for term_part in cheb_terms]) * grad_scale
    bias_grad = lax.optimization_barrier(jnp.sum(grad_maps, axis=(0, 1))) * grad_scale
    return (output, input_grad, weight_grad, bias_grad)
```

```python
import math

import jax
import jax.numpy as jnp
from jax import lax
from jax.experimental import pallas as pl
from jax.experimental.pallas import tpu as pltpu
from jax.sharding import Mesh
from jax.sharding import PartitionSpec as P

C = 64
BATCH = 2
PB = 64
NB = 6
HB = 4
BLK_DEV = 16
ROWS = BLK_DEV * PB
RIM = HB * PB
EXT = BLK_DEV + 2 * HB
W2 = BATCH * C
CHUNKS = PB * PB // 128
AXES = ("patch_0", "patch_1", "patch_2", "strip")
SHAPE = (4, 8, 4, 2)
BLOCKS = 4096
F32 = jnp.float32
BF16 = jnp.bfloat16
VMEM = pl.BlockSpec(memory_space=pltpu.VMEM)
SMEM = pl.BlockSpec(memory_space=pltpu.SMEM)
ANY = pl.BlockSpec(memory_space=pl.ANY)


def split(value):
    high = value.astype(BF16)
    return high, (value - high.astype(F32)).astype(BF16)


def mm(a, b):
    return jnp.dot(a, b, preferred_element_type=F32)


def mm_tn(a, b):
    return lax.dot_general(a, b, (((0,), (0,)), ((), ())), preferred_element_type=F32)


def slot_of(cols, b, j):
    return jnp.bitwise_and(cols[b, j] - cols[0, 0] + HB, BLOCKS - 1)


def is_first_core(cols):
    return jnp.bitwise_and(cols[0, 0] // BLK_DEV, 1) == 0


def rim_rows(cols):
    first = is_first_core(cols)
    low, high = 0, (BLK_DEV + HB) * PB
    return (
        pl.multiple_of(jnp.where(first, high, low), RIM),
        pl.multiple_of(jnp.where(first, low, high), RIM),
    )


def even_odd(ref, b):
    return jnp.concatenate(
        [ref[pl.ds(b * PB, PB // 2, stride=2), :], ref[pl.ds(b * PB + 1, PB // 2, stride=2), :]],
        axis=0,
    )


def spread(cols, at_ref, vec_ref, acc):
    def one(b, carry):
        high, low = split(even_odd(vec_ref, b))
        rhs = jnp.concatenate([high, high, low, low], axis=0)
        at = at_ref[b]
        out = mm(jnp.concatenate([at, at], axis=1), rhs)
        for j in range(NB):
            rows = pl.ds(pl.multiple_of(slot_of(cols, b, j) * PB, PB), PB)
            acc[rows, :] = acc[rows, :] + out[j * PB : (j + 1) * PB]
        return carry

    lax.fori_loop(0, BLK_DEV, one, 0, unroll=4)


def hop(cols, fa_ref, cat, out_ref):
    def one(b, carry):
        rhs = jnp.concatenate(
            [
                cat[pl.ds(pl.multiple_of(slot_of(cols, b, j) * PB, PB), PB), :]
                for j in range(NB)
            ],
            axis=0,
        )
        out = mm(fa_ref[b], rhs)
        out = out[:, :W2] + out[:, W2:]
        out = out[:PB] + out[PB:]
        out_ref[pl.ds(b * PB, PB // 2, stride=2), :] = out[: PB // 2]
        out_ref[pl.ds(b * PB + 1, PB // 2, stride=2), :] = out[PB // 2 :]
        return carry

    lax.fori_loop(0, BLK_DEV, one, 0, unroll=4)


def put_cat(cat, start, value):
    high, low = split(value)
    cat[pl.ds(start, value.shape[0]), :] = jnp.concatenate([high, low], axis=1)


def build_kernel(cols, tiles, g_ref, fa_ref, at_ref, u_ref, send_a, send_b, raw, acc, sem):
    copies = [
        pltpu.make_async_copy(
            tiles.at[:, :, pl.ds(k * 128, 128)], raw.at[:, pl.ds(8 * k, NB), :], sem.at[k]
        )
        for k in range(CHUNKS)
    ]
    for copy in copies:
        copy.start()
    acc[...] = jnp.zeros_like(acc)
    for copy in copies:
        copy.wait()
    low_lanes = lax.broadcasted_iota(jnp.int32, (CHUNKS, 128), 1) < PB

    def one(b, carry):
        for pair in range(NB // 2):
            even = raw[b, pl.ds(2 * pair, CHUNKS, stride=8), :]
            odd = raw[b, pl.ds(2 * pair + 1, CHUNKS, stride=8), :]
            top = jnp.where(low_lanes, even, pltpu.roll(odd, PB, 1))
            bottom = jnp.where(low_lanes, pltpu.roll(even, PB, 1), odd)
            both = jnp.concatenate([top, bottom], axis=0)
            high = both.astype(BF16)
            rest = both - high.astype(F32)
            low = rest.astype(BF16)
            lanes = pl.ds(pair * 128, 128)
            stacked = jnp.concatenate([high, low], axis=0)
            fa_ref[b, :, lanes] = stacked
            at_ref[b, lanes, :] = stacked.astype(F32).T.astype(BF16)
        return carry

    lax.fori_loop(0, BLK_DEV, one, 0, unroll=4)
    spread(cols, at_ref, g_ref, acc)
    u_ref[...] = acc[RIM : RIM + ROWS, :]
    row_a, row_b = rim_rows(cols)
    send_a[...] = acc[pl.ds(row_a, RIM), :]
    send_b[...] = acc[pl.ds(row_b, RIM), :]


def maps_sum(full):
    return full[:C] + pltpu.roll(full[C:], C, 1)


def first_kernel(cols, fa_ref, x_ref, x_a, x_b, g_ref, u_ref, first_ref, grads_ref, cat, *, scale):
    row_a, row_b = rim_rows(cols)
    put_cat(cat, RIM, x_ref[...])
    put_cat(cat, row_a, x_a[...])
    put_cat(cat, row_b, x_b[...])
    hop(cols, fa_ref, cat, first_ref)
    g_high, g_low = split(g_ref[...])
    u_high, u_low = split(u_ref[...])
    f_high, f_low = split(first_ref[...])
    xs = cat[RIM : RIM + ROWS, :]
    gs = jnp.concatenate([g_high, g_low], axis=1)
    gus = jnp.concatenate([g_high, g_low, u_high, u_low], axis=1)
    zero = mm_tn(xs, gs)
    zero = zero[:W2] + zero[W2:]
    zero = zero[:, :W2] + zero[:, W2:]
    rest = mm_tn(jnp.concatenate([f_high, f_low], axis=1), gus)
    rest = rest[:W2] + rest[W2:]
    one = rest[:, :W2] + rest[:, W2 : 2 * W2]
    two = 2.0 * (rest[:, 2 * W2 : 3 * W2] + rest[:, 3 * W2 :]) - zero
    low_lanes = lax.broadcasted_iota(jnp.int32, (C, 128), 1) < C
    zero, one, two = maps_sum(zero), maps_sum(one), maps_sum(two)
    grads_ref[0:C, :] = scale * jnp.where(low_lanes, zero, pltpu.roll(one, C, 1))
    half = C // 2
    grads_ref[C : C + half, :] = scale * jnp.where(
        low_lanes[:half], two[:half], pltpu.roll(two[half:], C, 1)
    )
    bias = jnp.sum(g_ref[...], axis=0, keepdims=True)
    grads_ref[C + half : C + half + 8, :] = jnp.broadcast_to(
        scale * (bias + pltpu.roll(bias, C, 1)), (8, 128)
    )


def grads_kernel(cols, first_ref, u_a, u_b, part_ref, grads_ref, *, scale):
    row_a, row_b = rim_rows(cols)
    total = jnp.zeros((W2, W2), F32)
    for row, u in ((row_a, u_a), (row_b, u_b)):
        own = pl.multiple_of(jnp.where(row == 0, 0, ROWS - RIM), RIM)
        f_high, f_low = split(first_ref[pl.ds(own, RIM), :])
        u_high, u_low = split(u[...])
        out = mm_tn(
            jnp.concatenate([f_high, f_low], axis=1), jnp.concatenate([u_high, u_low], axis=1)
        )
        out = out[:W2] + out[W2:]
        total = total + out[:, :W2] + out[:, W2:]
    two = (2.0 * scale) * maps_sum(total)
    half = C // 2
    low_lanes = lax.broadcasted_iota(jnp.int32, (half, 128), 1) < C
    grads_ref[...] = part_ref[...]
    grads_ref[C : C + half, :] = part_ref[C : C + half, :] + jnp.where(
        low_lanes, two[:half], pltpu.roll(two[half:], C, 1)
    )


def both_maps(weight):
    zero = jnp.zeros_like(weight)
    return jnp.concatenate(
        [jnp.concatenate([weight, zero], axis=1), jnp.concatenate([zero, weight], axis=1)], axis=0
    )


def mixed(value, weight):
    high, low = split(value)
    w_high, w_low = split(weight)
    row = jnp.concatenate([w_high, w_low], axis=1)
    out = mm(jnp.concatenate([high, low], axis=1), jnp.concatenate([row, row], axis=0))
    return out[:, :W2] + out[:, W2:]


def inner_kernel(
    cols, at_ref, g_ref, u_ref, u_a, u_b, w_ref, first_ref, u2_ref, send_a, send_b, inner, acc
):
    row_a, row_b = rim_rows(cols)
    inner[...] = u_ref[...]
    for row, u in ((row_a, u_a), (row_b, u_b)):
        own = pl.multiple_of(jnp.where(row == 0, 0, ROWS - RIM), RIM)
        inner[pl.ds(own, RIM), :] = inner[pl.ds(own, RIM), :] + u[...]
    inner[...] = mixed(g_ref[...], both_maps(w_ref[1]).T) + 2.0 * mixed(
        inner[...], both_maps(w_ref[2]).T
    )
    acc[...] = jnp.zeros_like(acc)
    spread(cols, at_ref, inner, acc)
    u2_ref[...] = acc[RIM : RIM + ROWS, :]
    for row, send in ((row_a, send_a), (row_b, send_b)):
        own = pl.multiple_of(jnp.where(row == 0, 0, ROWS - RIM), RIM)
        send[0:RIM, :] = first_ref[pl.ds(own, RIM), :]
        send[RIM : 2 * RIM, :] = acc[pl.ds(row, RIM), :]


def last_kernel(
    cols, fa_ref, x_ref, g_ref, first_ref, u2_ref, r_a, r_b, w_ref, bias_ref,
    out_ref, back_ref, cat, second,
):
    row_a, row_b = rim_rows(cols)
    put_cat(cat, RIM, first_ref[...])
    put_cat(cat, row_a, r_a[0:RIM, :])
    put_cat(cat, row_b, r_b[0:RIM, :])
    hop(cols, fa_ref, cat, second)
    x = x_ref[...]
    two = 2.0 * second[...] - x
    bias = bias_ref[...]
    out_ref[...] = (
        mixed(x, both_maps(w_ref[0]))
        + mixed(first_ref[...], both_maps(w_ref[1]))
        + mixed(two, both_maps(w_ref[2]))
        + jnp.concatenate([bias, bias], axis=1)
    )
    g = g_ref[...]
    back_ref[...] = u2_ref[...] + mixed(g, both_maps(w_ref[0] - w_ref[2]).T)
    for row, r in ((row_a, r_a), (row_b, r_b)):
        own = pl.multiple_of(jnp.where(row == 0, 0, ROWS - RIM), RIM)
        back_ref[pl.ds(own, RIM), :] = back_ref[pl.ds(own, RIM), :] + r[RIM : 2 * RIM, :]


def call(kernel, name, out, specs, scratch, flops, moved):
    return pl.pallas_call(
        kernel,
        name=name,
        out_shape=[jax.ShapeDtypeStruct(s, d) for s, d in out],
        in_specs=specs,
        out_specs=[VMEM] * len(out),
        scratch_shapes=scratch,
        compiler_params=pltpu.CompilerParams(vmem_limit_bytes=32 * 1024 * 1024),
        cost_estimate=pl.CostEstimate(flops=flops, bytes_accessed=moved, transcendentals=0),
    )


def index(a, b, c, s):
    return ((a * SHAPE[1] + b) * SHAPE[2] + c) * SHAPE[3] + s


def place(i):
    return (i // 64, (i // 8) % 8, (i // 2) % 4, i % 2)


COUNT = 256
IN_CHIP = [(i, i ^ 1) for i in range(COUNT)]
CROSS = [(i, (i + 1) % COUNT) if i % 2 else (i, (i - 1) % COUNT) for i in range(COUNT)]
RING4 = ((1, 0, 3, 2), (3, 2, 1, 0))
RING8 = ((1, 0, 3, 2, 5, 4, 7, 6), (7, 2, 1, 4, 3, 6, 5, 0), (3, 6, 5, 0, 7, 2, 1, 4))


def moves():
    steps = [IN_CHIP]
    for table in RING4:
        steps.append([(i, index(a, b, table[c], s)) for i, (a, b, c, s) in enumerate(map(place, range(COUNT)))])
    for table in RING4:
        steps.append([(i, index(table[a], b, c, s)) for i, (a, b, c, s) in enumerate(map(place, range(COUNT)))])
    for table in RING8:
        steps.append([(i, index(a, table[b], c, s)) for i, (a, b, c, s) in enumerate(map(place, range(COUNT)))])
    return steps


def shards(features, lap_tiles, columns, weights, bias_term, cotangent):
    scale = 1.0 / math.sqrt(BATCH * PB * BLOCKS)
    first_core = lax.axis_index("strip") == 0
    x_a = lax.dynamic_slice_in_dim(features, jnp.where(first_core, ROWS - RIM, 0), RIM, 0)
    x_b = lax.dynamic_slice_in_dim(features, jnp.where(first_core, 0, ROWS - RIM), RIM, 0)
    x_b = lax.ppermute(x_b, AXES, CROSS)
    x_a = lax.ppermute(x_a, AXES, IN_CHIP)
    field = ((ROWS, W2), F32)
    rim = ((RIM, W2), F32)
    fa, at, u, u_a, u_b = call(
        build_kernel, "build",
        [((BLK_DEV, 2 * PB, NB * PB), BF16), ((BLK_DEV, NB * PB, 2 * PB), BF16), field, rim, rim],
        [SMEM, ANY, VMEM],
        [
            pltpu.VMEM((BLK_DEV, CHUNKS * 8, 128), F32),
            pltpu.VMEM((EXT * PB, W2), F32),
            pltpu.SemaphoreType.DMA((CHUNKS,)),
        ],
        800_000_000, 8_000_000,
    )(columns, lap_tiles, cotangent)
    u_b = lax.ppermute(u_b, AXES, CROSS)
    u_a = lax.ppermute(u_a, AXES, IN_CHIP)

    def first_body(*refs):
        first_kernel(*refs, scale=scale)

    first, part = call(
        first_body, "first", [field, ((C + C // 2 + 8, W2), F32)],
        [SMEM] + [VMEM] * 6, [pltpu.VMEM((EXT * PB, 2 * W2), BF16)], 800_000_000, 4_000_000,
    )(columns, fa, features, x_a, x_b, cotangent, u)

    def grads_body(*refs):
        grads_kernel(*refs, scale=scale)

    (grads,) = call(
        grads_body, "grads", [((C + C // 2 + 8, W2), F32)], [SMEM] + [VMEM] * 4, [],
        50_000_000, 500_000,
    )(columns, first, u_a, u_b, part)
    for step in moves()[:1]:
        grads = grads + lax.ppermute(grads, AXES, step)
    u2, s_a, s_b = call(
        inner_kernel, "inner", [field, ((2 * RIM, W2), F32), ((2 * RIM, W2), F32)],
        [SMEM] + [VMEM] * 7,
        [pltpu.VMEM((ROWS, W2), F32), pltpu.VMEM((EXT * PB, W2), F32)], 800_000_000, 4_000_000,
    )(columns, at, cotangent, u, u_a, u_b, weights, first)
    s_b = lax.ppermute(s_b, AXES, CROSS)
    s_a = lax.ppermute(s_a, AXES, IN_CHIP)
    output, input_grad = call(
        last_kernel, "last", [field, field], [SMEM] + [VMEM] * 9,
        [pltpu.VMEM((EXT * PB, 2 * W2), BF16), pltpu.VMEM((ROWS, W2), F32)],
        800_000_000, 5_000_000,
    )(columns, fa, features, cotangent, first, u2, s_a, s_b, weights, bias_term.reshape(1, C))
    for step in moves()[1:]:
        grads = grads + lax.ppermute(grads, AXES, step)
    half = C // 2
    weight_grad = jnp.stack(
        [
            grads[:C, :C],
            grads[:C, C:],
            jnp.concatenate([grads[C : C + half, :C], grads[C : C + half, C:]], axis=0),
        ]
    )
    return output, input_grad, weight_grad, grads[C + half, :C]


def solution(mesh):
    grid = Mesh(mesh.devices.reshape(*SHAPE), AXES)
    placed = (P(AXES, None), P(AXES, None, None), P(AXES, None), P(), P(), P(AXES, None))
    return jax.shard_map(
        shards,
        mesh=grid,
        in_specs=placed,
        out_specs=(P(AXES, None), P(AXES, None), P(), P()),
        check_vma=False,
    )
```

```python
import math

import jax
import jax.numpy as jnp
from jax import lax
from jax.experimental import pallas as pl
from jax.experimental.pallas import tpu as pltpu
from jax.sharding import Mesh
from jax.sharding import PartitionSpec as P

C = 64
BATCH = 2
PB = 64
NB = 6
HB = 4
BLK_DEV = 16
ROWS = BLK_DEV * PB
RIM = HB * PB
EXT = BLK_DEV + 2 * HB
MID = BLK_DEV - 2 * HB
W2 = BATCH * C
CHUNKS = PB * PB // 128
AXES = ("patch_0", "patch_1", "patch_2", "strip")
SHAPE = (4, 8, 4, 2)
BLOCKS = 4096
F32 = jnp.float32
BF16 = jnp.bfloat16
VMEM = pl.BlockSpec(memory_space=pltpu.VMEM)
SMEM = pl.BlockSpec(memory_space=pltpu.SMEM)
HBM = pl.BlockSpec(memory_space=pltpu.HBM)


def split(value):
    high = value.astype(BF16)
    return high, (value - high.astype(F32)).astype(BF16)


def mm(a, b):
    return jnp.dot(a, b, preferred_element_type=F32)


def mm_tn(a, b):
    return lax.dot_general(a, b, (((0,), (0,)), ((), ())), preferred_element_type=F32)


def slot_of(cols, b, j):
    return jnp.bitwise_and(cols[b, j] - cols[0, 0] + HB, BLOCKS - 1)


def is_first_core(cols):
    return jnp.bitwise_and(cols[0, 0] // BLK_DEV, 1) == 0


def rim_rows(cols):
    first = is_first_core(cols)
    low, high = 0, (BLK_DEV + HB) * PB
    return (
        pl.multiple_of(jnp.where(first, high, low), RIM),
        pl.multiple_of(jnp.where(first, low, high), RIM),
    )


def rim_half(row):
    return pl.multiple_of(jnp.where(row == 0, 0, RIM), RIM)


def rim_block(i):
    return jnp.where(i < HB, i, i + MID)


def mid_block(i):
    return i + HB


def block_rows(ref, i):
    return jnp.concatenate(
        [ref[pl.ds(i * PB, PB // 2, stride=2), :], ref[pl.ds(i * PB + 1, PB // 2, stride=2), :]],
        axis=0,
    )


def rows_of(slot):
    return pl.ds(pl.multiple_of(slot * PB, PB), PB)


def spread(cols, at_ref, vec_ref, acc, block):
    def one(i, carry):
        b = block(i)
        high, low = split(block_rows(vec_ref, i))
        rhs = jnp.concatenate([high, high, low, low], axis=0)
        at = at_ref[i]
        out = mm(jnp.concatenate([at, at], axis=1), rhs)
        for j in range(NB):
            rows = rows_of(slot_of(cols, b, j))
            acc[rows, :] = acc[rows, :] + out[j * PB : (j + 1) * PB]
        return carry

    lax.fori_loop(0, MID, one, 0, unroll=4)


def hop(cols, fa_ref, cat, out_ref, block):
    def one(i, carry):
        b = block(i)
        rhs = jnp.concatenate([cat[rows_of(slot_of(cols, b, j)), :] for j in range(NB)], axis=0)
        out = mm(fa_ref[i], rhs)
        out = out[:, :W2] + out[:, W2:]
        out = out[:PB] + out[PB:]
        out_ref[pl.ds(i * PB, PB // 2, stride=2), :] = out[: PB // 2]
        out_ref[pl.ds(i * PB + 1, PB // 2, stride=2), :] = out[PB // 2 :]
        return carry

    lax.fori_loop(0, MID, one, 0, unroll=4)


def put_cat(cat, start, value):
    high, low = split(value)
    cat[pl.ds(start, value.shape[0]), :] = jnp.concatenate([high, low], axis=1)


def build(raw, fa_ref, at_ref):
    low_lanes = lax.broadcasted_iota(jnp.int32, (CHUNKS, 128), 1) < PB

    def one(i, carry):
        for pair in range(NB // 2):
            even = raw[i, pl.ds(2 * pair, CHUNKS, stride=8), :]
            odd = raw[i, pl.ds(2 * pair + 1, CHUNKS, stride=8), :]
            top = jnp.where(low_lanes, even, pltpu.roll(odd, PB, 1))
            bottom = jnp.where(low_lanes, pltpu.roll(even, PB, 1), odd)
            both = jnp.concatenate([top, bottom], axis=0)
            high = both.astype(BF16)
            low = (both - high.astype(F32)).astype(BF16)
            lanes = pl.ds(pair * 128, 128)
            stacked = jnp.concatenate([high, low], axis=0)
            fa_ref[i, :, lanes] = stacked
            at_ref[i, lanes, :] = stacked.astype(F32).T.astype(BF16)
        return carry

    lax.fori_loop(0, MID, one, 0, unroll=4)


def tile_copies(tiles, raw, sem, pieces):
    return [
        pltpu.make_async_copy(
            tiles.at[pl.ds(start, count), :, pl.ds(k * 128, 128)],
            raw.at[pl.ds(at, count), pl.ds(8 * k, NB), :],
            sem.at[n * CHUNKS + k],
        )
        for n, (start, count, at) in enumerate(pieces)
        for k in range(CHUNKS)
    ]


def rim_kernel(
    cols_hbm, tiles, g_hbm, x_hbm,
    cols_ref, fa_ref, at_ref, acc, send_a, send_b,
    cols, raw, g_rim, x_rim, sem, small,
):
    to_cols = pltpu.make_async_copy(cols_hbm, cols, small.at[0])
    others = [pltpu.make_async_copy(cols_hbm, cols_ref, small.at[1])]
    for n, (value, to) in enumerate(((g_hbm, g_rim), (x_hbm, x_rim))):
        others.append(
            pltpu.make_async_copy(value.at[pl.ds(0, RIM)], to.at[pl.ds(0, RIM)], small.at[2 + 2 * n])
        )
        others.append(
            pltpu.make_async_copy(
                value.at[pl.ds(ROWS - RIM, RIM)], to.at[pl.ds(RIM, RIM)], small.at[3 + 2 * n]
            )
        )
    copies = tile_copies(tiles, raw, sem, ((0, HB, 0), (BLK_DEV - HB, HB, HB)))
    for copy in copies + [to_cols] + others:
        copy.start()
    acc[...] = jnp.zeros_like(acc)
    for copy in copies:
        copy.wait()
    build(raw, fa_ref, at_ref)
    to_cols.wait()
    for copy in others:
        copy.wait()
    spread(cols, at_ref, g_rim, acc, rim_block)
    for row, send in zip(rim_rows(cols), (send_a, send_b)):
        send[0:RIM, :] = x_rim[pl.ds(rim_half(row), RIM), :]
        send[RIM : 2 * RIM, :] = acc[pl.ds(row, RIM), :]


def maps_sum(full):
    return full[:C] + pltpu.roll(full[C:], C, 1)


def products(left, right):
    a = jnp.concatenate([h for value in left for h in split(value)], axis=1)
    b = jnp.concatenate([h for value in right for h in split(value)], axis=1)
    out = mm_tn(a, b)
    result = []
    for p in range(len(left)):
        band = out[2 * p * W2 : (2 * p + 1) * W2] + out[(2 * p + 1) * W2 : (2 * p + 2) * W2]
        result.append(
            [
                band[:, 2 * q * W2 : (2 * q + 1) * W2] + band[:, (2 * q + 1) * W2 : (2 * q + 2) * W2]
                for q in range(len(right))
            ]
        )
    return result


def packed(zero, one, two):
    low_lanes = lax.broadcasted_iota(jnp.int32, (C, 128), 1) < C
    two = maps_sum(two)
    one = pltpu.roll(maps_sum(one), C, 1)
    if zero is None:
        top = jnp.where(low_lanes, 0.0, one)
    else:
        top = jnp.where(low_lanes, maps_sum(zero), one)
    bottom = jnp.where(low_lanes[: C // 2], two[: C // 2], pltpu.roll(two[C // 2 :], C, 1))
    return jnp.concatenate([top, bottom], axis=0)


def both_maps(weight):
    zero = jnp.zeros_like(weight)
    return jnp.concatenate(
        [jnp.concatenate([weight, zero], axis=1), jnp.concatenate([zero, weight], axis=1)], axis=0
    )


def mixed(value, weight):
    high, low = split(value)
    w_high, w_low = split(weight)
    row = jnp.concatenate([w_high, w_low], axis=1)
    out = mm(jnp.concatenate([high, low], axis=1), jnp.concatenate([row, row], axis=0))
    return out[:, :W2] + out[:, W2:]


def mid_kernel(
    cols, tiles, g_ref, x_ref, acc_in, w_ref,
    fa_ref, at_ref, first_ref, u_rim, part_ref, acc,
    raw, cat, inner, u_mid, sem, *, scale,
):
    copies = tile_copies(tiles, raw, sem, ((HB, MID, 0),))
    for copy in copies:
        copy.start()
    put_cat(cat, RIM, x_ref[...])
    acc[...] = acc_in[...]
    for copy in copies:
        copy.wait()
    build(raw, fa_ref, at_ref)
    g_mid = g_ref.at[pl.ds(RIM, MID * PB)]
    spread(cols, at_ref, g_mid, acc, mid_block)
    u_mid[...] = acc[2 * RIM : 4 * RIM, :]
    u_rim[0:RIM, :] = acc[RIM : 2 * RIM, :]
    u_rim[RIM : 2 * RIM, :] = acc[4 * RIM : 5 * RIM, :]
    hop(cols, fa_ref, cat, first_ref, mid_block)
    inner[...] = mixed(g_mid[...], both_maps(w_ref[1]).T) + 2.0 * mixed(
        u_mid[...], both_maps(w_ref[2]).T
    )
    acc[...] = jnp.zeros_like(acc)
    spread(cols, at_ref, inner, acc, mid_block)
    ((zero,),) = products([x_ref[...]], [g_ref[...]])
    ((one, two),) = products([first_ref[...]], [g_mid[...], u_mid[...]])
    part_ref[0 : C + C // 2, :] = scale * packed(zero, one, 2.0 * two - zero)
    bias = scale * jnp.sum(g_ref[...], axis=0, keepdims=True)
    part_ref[C + C // 2 :, :] = jnp.broadcast_to(bias + pltpu.roll(bias, C, 1), (8, 128))


def meet_kernel(
    cols, fa_ref, x_ref, r_a, r_b, g_ref, u_part, part_ref, first_ref, u_ref, grads_ref, cat, *, scale
):
    put_cat(cat, RIM, x_ref[...])
    for row, r in zip(rim_rows(cols), (r_a, r_b)):
        put_cat(cat, row, r[0:RIM, :])
        half = pl.ds(rim_half(row), RIM)
        u_ref[half, :] = u_part[half, :] + r[RIM : 2 * RIM, :]
    hop(cols, fa_ref, cat, first_ref, rim_block)
    g_rim = jnp.concatenate([g_ref[0:RIM, :], g_ref[ROWS - RIM :, :]], axis=0)
    ((one, two),) = products([first_ref[...]], [g_rim, u_ref[...]])
    size = C + C // 2
    grads_ref[0:size, :] = part_ref[0:size, :] + scale * packed(None, one, 2.0 * two)
    grads_ref[size:, :] = part_ref[size:, :]


def inner_kernel(
    cols, at_ref, g_ref, u_ref, w_ref, first_ref, acc_in, u2_ref, send_a, send_b, inner, acc
):
    g_rim = jnp.concatenate([g_ref[0:RIM, :], g_ref[ROWS - RIM :, :]], axis=0)
    inner[...] = mixed(g_rim, both_maps(w_ref[1]).T) + 2.0 * mixed(
        u_ref[...], both_maps(w_ref[2]).T
    )
    acc[...] = acc_in[...]
    spread(cols, at_ref, inner, acc, rim_block)
    u2_ref[...] = acc[RIM : RIM + ROWS, :]
    for row, send in zip(rim_rows(cols), (send_a, send_b)):
        send[0:RIM, :] = first_ref[pl.ds(rim_half(row), RIM), :]
        send[RIM : 2 * RIM, :] = acc[pl.ds(row, RIM), :]


def outputs(x, g, one, hopped, w_ref, bias_ref):
    bias = bias_ref[...]
    out = (
        mixed(x, both_maps(w_ref[0]))
        + mixed(one, both_maps(w_ref[1]))
        + mixed(2.0 * hopped - x, both_maps(w_ref[2]))
        + jnp.concatenate([bias, bias], axis=1)
    )
    return out, mixed(g, both_maps(w_ref[0] - w_ref[2]).T)


def last_mid_kernel(
    cols, fa_ref, x_ref, g_ref, f_mid, f_rim, u2_ref, w_ref, bias_ref, out_ref, back_ref, cat, second
):
    put_cat(cat, RIM, f_rim[0:RIM, :])
    put_cat(cat, 2 * RIM, f_mid[...])
    put_cat(cat, 4 * RIM, f_rim[RIM : 2 * RIM, :])
    hop(cols, fa_ref, cat, second, mid_block)
    mid = slice(RIM, ROWS - RIM)
    out, back = outputs(x_ref[mid, :], g_ref[mid, :], f_mid[...], second[...], w_ref, bias_ref)
    out_ref[...] = out
    back_ref[...] = back + u2_ref[mid, :]


def last_rim_kernel(
    cols, fa_ref, x_ref, g_ref, f_mid, f_rim, r_a, r_b, u2_ref, w_ref, bias_ref, o_mid, b_mid,
    out_ref, back_ref, cat, second,
):
    put_cat(cat, RIM, f_rim[0:RIM, :])
    put_cat(cat, 2 * RIM, f_mid[...])
    put_cat(cat, 4 * RIM, f_rim[RIM : 2 * RIM, :])
    for row, r in zip(rim_rows(cols), (r_a, r_b)):
        put_cat(cat, row, r[0:RIM, :])
    hop(cols, fa_ref, cat, second, rim_block)
    x = jnp.concatenate([x_ref[0:RIM, :], x_ref[ROWS - RIM :, :]], axis=0)
    g = jnp.concatenate([g_ref[0:RIM, :], g_ref[ROWS - RIM :, :]], axis=0)
    out, back = outputs(x, g, f_rim[...], second[...], w_ref, bias_ref)
    mid = slice(RIM, ROWS - RIM)
    out_ref[mid, :] = o_mid[...]
    back_ref[mid, :] = b_mid[...]
    for at, half in ((0, 0), (ROWS - RIM, RIM)):
        out_ref[at : at + RIM, :] = out[half : half + RIM]
        back_ref[at : at + RIM, :] = back[half : half + RIM] + u2_ref[at : at + RIM, :]
    for row, r in zip(rim_rows(cols), (r_a, r_b)):
        own = pl.ds(pl.multiple_of(jnp.where(row == 0, 0, ROWS - RIM), RIM), RIM)
        back_ref[own, :] = back_ref[own, :] + r[RIM : 2 * RIM, :]


def final_kernel(mine, theirs, weight_ref, bias_ref):
    total = mine[...] + theirs[...]
    half = C // 2
    weight_ref[0] = total[:C, :C]
    weight_ref[1] = pltpu.roll(total[:C], C, 1)[:, :C]
    weight_ref[2, 0:half, :] = total[C : C + half, :C]
    weight_ref[2, half:C, :] = pltpu.roll(total[C : C + half], C, 1)[:, :C]
    bias_ref[...] = total[C + half : C + half + 1, :C]


def call(kernel, name, out, specs, scratch, flops, moved):
    return pl.pallas_call(
        kernel,
        name=name,
        out_shape=[jax.ShapeDtypeStruct(s, d) for s, d in out],
        in_specs=specs,
        out_specs=[VMEM] * len(out),
        scratch_shapes=scratch,
        compiler_params=pltpu.CompilerParams(vmem_limit_bytes=24 * 1024 * 1024),
        cost_estimate=pl.CostEstimate(flops=flops, bytes_accessed=moved, transcendentals=0),
    )


def index(a, b, c, s):
    return ((a * SHAPE[1] + b) * SHAPE[2] + c) * SHAPE[3] + s


def place(i):
    return (i // 64, (i // 8) % 8, (i // 2) % 4, i % 2)


COUNT = 256
IN_CHIP = [(i, i ^ 1) for i in range(COUNT)]
CROSS = [(i, (i + 1) % COUNT) if i % 2 else (i, (i - 1) % COUNT) for i in range(COUNT)]
RING4 = ((1, 0, 3, 2), (3, 2, 1, 0))
RING8 = ((1, 0, 3, 2, 5, 4, 7, 6), (7, 2, 1, 4, 3, 6, 5, 0), (3, 6, 5, 0, 7, 2, 1, 4))


def moves():
    steps = [IN_CHIP]
    for table in RING4:
        steps.append([(i, index(a, b, table[c], s)) for i, (a, b, c, s) in enumerate(map(place, range(COUNT)))])
    for table in RING4:
        steps.append([(i, index(table[a], b, c, s)) for i, (a, b, c, s) in enumerate(map(place, range(COUNT)))])
    for table in RING8:
        steps.append([(i, index(a, table[b], c, s)) for i, (a, b, c, s) in enumerate(map(place, range(COUNT)))])
    return steps


def shards(features, lap_tiles, columns, weights, bias_term, cotangent):
    scale = 1.0 / math.sqrt(BATCH * PB * BLOCKS)
    field = ((ROWS, W2), F32)
    half = ((ROWS // 2, W2), F32)
    extended = ((EXT * PB, W2), F32)
    sums = ((C + C // 2 + 8, W2), F32)
    natural = ((MID, 2 * PB, NB * PB), BF16)
    turned = ((MID, NB * PB, 2 * PB), BF16)
    raw = pltpu.VMEM((MID, CHUNKS * 8, 128), F32)
    cat = pltpu.VMEM((EXT * PB, 2 * W2), BF16)
    half_scratch = pltpu.VMEM((ROWS // 2, W2), F32)

    def scaled(kernel):
        def body(*refs):
            kernel(*refs, scale=scale)

        return body

    cols, fa_rim, at_rim, acc, s_a, s_b = call(
        rim_kernel, "rim", [((BLK_DEV, NB), jnp.int32), natural, turned, extended, half, half],
        [HBM] * 4,
        [
            pltpu.SMEM((BLK_DEV, NB), jnp.int32), raw, half_scratch, half_scratch,
            pltpu.SemaphoreType.DMA((2 * CHUNKS,)), pltpu.SemaphoreType.DMA((6,)),
        ],
        400_000_000, 4_000_000,
    )(columns, lap_tiles, cotangent, features)
    r_b = lax.ppermute(s_b, AXES, CROSS)
    r_a = lax.ppermute(s_a, AXES, IN_CHIP)
    fa_mid, at_mid, f_mid, u_rim, part, acc = call(
        scaled(mid_kernel), "mid", [natural, turned, half, half, sums, extended],
        [SMEM, HBM] + [VMEM] * 4,
        [raw, cat, half_scratch, half_scratch, pltpu.SemaphoreType.DMA((CHUNKS,))],
        1_600_000_000, 9_000_000,
    )(cols, lap_tiles, cotangent, features, acc, weights)
    f_rim, u_rim, grads = call(
        scaled(meet_kernel), "meet", [half, half, sums], [SMEM] + [VMEM] * 7, [cat],
        400_000_000, 3_000_000,
    )(cols, fa_rim, features, r_a, r_b, cotangent, u_rim, part)
    steps = moves()
    grads = grads + lax.ppermute(grads, AXES, steps[0])
    u2, s_a, s_b = call(
        inner_kernel, "inner", [field, half, half], [SMEM] + [VMEM] * 6,
        [half_scratch, pltpu.VMEM(*extended)], 400_000_000, 3_000_000,
    )(cols, at_rim, cotangent, u_rim, weights, f_rim, acc)
    s_b = lax.ppermute(s_b, AXES, CROSS)
    s_a = lax.ppermute(s_a, AXES, IN_CHIP)
    bias_row = bias_term.reshape(1, C)
    o_mid, b_mid = call(
        last_mid_kernel, "last_mid", [half, half], [SMEM] + [VMEM] * 8, [cat, half_scratch],
        600_000_000, 4_000_000,
    )(cols, fa_mid, features, cotangent, f_mid, f_rim, u2, weights, bias_row)
    output, input_grad = call(
        last_rim_kernel, "last_rim", [field, field], [SMEM] + [VMEM] * 12, [cat, half_scratch],
        600_000_000, 5_000_000,
    )(cols, fa_rim, features, cotangent, f_mid, f_rim, s_a, s_b, u2, weights, bias_row, o_mid, b_mid)
    for step in steps[1:-1]:
        grads = grads + lax.ppermute(grads, AXES, step)
    weight_grad, bias_grad = call(
        final_kernel, "final", [((3, C, C), F32), ((1, C), F32)], [VMEM, VMEM], [], 1000, 100_000
    )(grads, lax.ppermute(grads, AXES, steps[-1]))
    return output, input_grad, weight_grad, bias_grad.reshape(C)


def solution(mesh):
    grid = Mesh(mesh.devices.reshape(*SHAPE), AXES)
    placed = (P(AXES, None), P(AXES, None, None), P(AXES, None), P(), P(), P(AXES, None))
    return jax.shard_map(
        shards,
        mesh=grid,
        in_specs=placed,
        out_specs=(P(AXES, None), P(AXES, None), P(), P()),
        check_vma=False,
    )
```

```python
import math

import jax
import jax.numpy as jnp
from jax import lax
from jax.experimental import pallas as pl
from jax.experimental.pallas import tpu as pltpu
from jax.sharding import Mesh
from jax.sharding import PartitionSpec as P


C = 64
BATCH = 2
PB = 64
NB = 6
HB = 4
BLK_DEV = 16
ROWS = BLK_DEV * PB
RIM = HB * PB
EXT = BLK_DEV + 2 * HB
MID = BLK_DEV - 2 * HB
HALF = 3 * C // 4
W2 = BATCH * C
CHUNKS = PB * PB // 128
AXES = ("patch_0", "patch_1", "patch_2", "strip")
SHAPE = (4, 8, 4, 2)
BLOCKS = 4096
F32 = jnp.float32
BF16 = jnp.bfloat16
VMEM = pl.BlockSpec(memory_space=pltpu.VMEM)
SMEM = pl.BlockSpec(memory_space=pltpu.SMEM)
HBM = pl.BlockSpec(memory_space=pltpu.HBM)


def split(value):
    high = value.astype(BF16)
    return high, (value - high.astype(F32)).astype(BF16)


def mm(a, b):
    return jnp.dot(a, b, preferred_element_type=F32)


def mm_tn(a, b):
    return lax.dot_general(a, b, (((0,), (0,)), ((), ())), preferred_element_type=F32)


def slot_of(cols, b, j):
    return jnp.bitwise_and(cols[j, b] - cols[0, 0] + HB, BLOCKS - 1)


def is_first_core(cols):
    return jnp.bitwise_and(cols[0, 0] // BLK_DEV, 1) == 0


def rim_rows(cols):
    first = is_first_core(cols)
    low, high = 0, (BLK_DEV + HB) * PB
    return (
        pl.multiple_of(jnp.where(first, high, low), RIM),
        pl.multiple_of(jnp.where(first, low, high), RIM),
    )


def rim_half(row):
    return pl.multiple_of(jnp.where(row == 0, 0, RIM), RIM)


def rim_block(i):
    return jnp.where(i < HB, i, i + MID)


def mid_block(i):
    return i + HB


def block_rows(ref, i):
    return jnp.concatenate(
        [ref[pl.ds(i * PB, PB // 2, stride=2), :], ref[pl.ds(i * PB + 1, PB // 2, stride=2), :]],
        axis=0,
    )


def rows_of(slot):
    return pl.ds(pl.multiple_of(slot * PB, PB), PB)


def spread(cols, at_ref, vec_ref, acc, block):
    def one(i, carry):
        b = block(i)
        high, low = split(block_rows(vec_ref, i))
        rhs = jnp.concatenate([high, high, low, low], axis=0)
        at = at_ref[i]
        out = mm(jnp.concatenate([at, at], axis=1), rhs)
        for j in range(NB):
            rows = rows_of(slot_of(cols, b, j))
            acc[rows, :] = acc[rows, :] + out[j * PB : (j + 1) * PB]
        return carry

    lax.fori_loop(0, MID, one, 0, unroll=4)


def hop(cols, fa_ref, cat, out_ref, block):
    def one(i, carry):
        b = block(i)
        rhs = jnp.concatenate([cat[rows_of(slot_of(cols, b, j)), :] for j in range(NB)], axis=0)
        out = mm(fa_ref[i], rhs)
        out = out[:, :W2] + out[:, W2:]
        out = out[:PB] + out[PB:]
        out_ref[pl.ds(i * PB, PB // 2, stride=2), :] = out[: PB // 2]
        out_ref[pl.ds(i * PB + 1, PB // 2, stride=2), :] = out[PB // 2 :]
        return carry

    lax.fori_loop(0, MID, one, 0, unroll=4)


def put_cat(cat, start, value):
    high, low = split(value)
    cat[pl.ds(start, value.shape[0]), :] = jnp.concatenate([high, low], axis=1)


def build(raw, fa_ref, at_ref, block):
    low_lanes = lax.broadcasted_iota(jnp.int32, (CHUNKS, 128), 1) < PB

    def one(i, carry):
        b = block(i)
        group, rows = b // 8, pl.ds(b % 8, CHUNKS, stride=8)
        for pair in range(NB // 2):
            even = raw[2 * pair, group, rows, :]
            odd = raw[2 * pair + 1, group, rows, :]
            top = jnp.where(low_lanes, even, pltpu.roll(odd, PB, 1))
            bottom = jnp.where(low_lanes, pltpu.roll(even, PB, 1), odd)
            both = jnp.concatenate([top, bottom], axis=0)
            high = both.astype(BF16)
            low = (both - high.astype(F32)).astype(BF16)
            lanes = pl.ds(pair * 128, 128)
            stacked = jnp.concatenate([high, low], axis=0)
            fa_ref[i, :, lanes] = stacked
            at_ref[i, lanes, :] = stacked.T
        return carry

    lax.fori_loop(0, MID, one, 0, unroll=4)


def rim_kernel(
    cols_hbm, tiles, g_hbm, x_hbm,
    cols_ref, raw, fa_ref, at_ref, acc, send_a, send_b,
    cols, g_rim, x_rim, sem, small,
):
    to_cols = pltpu.make_async_copy(cols_hbm, cols, small.at[0])
    others = [pltpu.make_async_copy(cols_hbm, cols_ref, small.at[1])]
    for n, (value, to) in enumerate(((g_hbm, g_rim), (x_hbm, x_rim))):
        others.append(
            pltpu.make_async_copy(value.at[pl.ds(0, RIM)], to.at[pl.ds(0, RIM)], small.at[2 + 2 * n])
        )
        others.append(
            pltpu.make_async_copy(
                value.at[pl.ds(ROWS - RIM, RIM)], to.at[pl.ds(RIM, RIM)], small.at[3 + 2 * n]
            )
        )
    copies = [
        pltpu.make_async_copy(
            tiles.at[:, pl.ds(8 * group, 8), pl.ds(k * 128, 128)],
            raw.at[:, group, pl.ds(8 * k, 8), :],
            sem.at[group * CHUNKS + k],
        )
        for group in range(BLK_DEV // 8)
        for k in range(CHUNKS)
    ]
    for copy in copies + [to_cols] + others:
        copy.start()
    acc[...] = jnp.zeros_like(acc)
    for copy in copies:
        copy.wait()
    build(raw, fa_ref, at_ref, rim_block)
    to_cols.wait()
    for copy in others:
        copy.wait()
    spread(cols, at_ref, g_rim, acc, rim_block)
    for row, send in zip(rim_rows(cols), (send_a, send_b)):
        send[0:RIM, :] = x_rim[pl.ds(rim_half(row), RIM), :]
        send[RIM : 2 * RIM, :] = acc[pl.ds(row, RIM), :]


def maps_sum(full):
    return full[:C] + pltpu.roll(full[C:], C, 1)


def products(left, right):
    a = jnp.concatenate([h for value in left for h in split(value)], axis=1)
    b = jnp.concatenate([h for value in right for h in split(value)], axis=1)
    out = mm_tn(a, b)
    result = []
    for p in range(len(left)):
        band = out[2 * p * W2 : (2 * p + 1) * W2] + out[(2 * p + 1) * W2 : (2 * p + 2) * W2]
        result.append(
            [
                band[:, 2 * q * W2 : (2 * q + 1) * W2] + band[:, (2 * q + 1) * W2 : (2 * q + 2) * W2]
                for q in range(len(right))
            ]
        )
    return result


def packed(zero, one, two):
    low_lanes = lax.broadcasted_iota(jnp.int32, (C, 128), 1) < C
    two = maps_sum(two)
    one = pltpu.roll(maps_sum(one), C, 1)
    if zero is None:
        top = jnp.where(low_lanes, 0.0, one)
    else:
        top = jnp.where(low_lanes, maps_sum(zero), one)
    bottom = jnp.where(low_lanes[: C // 2], two[: C // 2], pltpu.roll(two[C // 2 :], C, 1))
    return jnp.concatenate([top, bottom], axis=0)


def both_maps(weight):
    zero = jnp.zeros_like(weight)
    return jnp.concatenate(
        [jnp.concatenate([weight, zero], axis=1), jnp.concatenate([zero, weight], axis=1)], axis=0
    )


def mixed(value, weight):
    high, low = split(value)
    w_high, w_low = split(weight)
    row = jnp.concatenate([w_high, w_low], axis=1)
    out = mm(jnp.concatenate([high, low], axis=1), jnp.concatenate([row, row], axis=0))
    return out[:, :W2] + out[:, W2:]


def mid_kernel(
    cols, raw, g_ref, x_ref, acc_in,
    fa_ref, at_ref, first_ref, u_mid, u_rim, part_ref,
    cat, acc, *, scale,
):
    put_cat(cat, RIM, x_ref[...])
    acc[...] = acc_in[...]
    build(raw, fa_ref, at_ref, mid_block)
    g_mid = g_ref.at[pl.ds(RIM, MID * PB)]
    spread(cols, at_ref, g_mid, acc, mid_block)
    u_mid[...] = acc[2 * RIM : 4 * RIM, :]
    u_rim[0:RIM, :] = acc[RIM : 2 * RIM, :]
    u_rim[RIM : 2 * RIM, :] = acc[4 * RIM : 5 * RIM, :]
    hop(cols, fa_ref, cat, first_ref, mid_block)
    ((zero,),) = products([x_ref[...]], [g_ref[...]])
    ((one, two),) = products([first_ref[...]], [g_mid[...], u_mid[...]])
    part_ref[0 : C + C // 2, :] = scale * packed(zero, one, 2.0 * two - zero)
    bias = scale * jnp.sum(g_ref[...], axis=0, keepdims=True)
    part_ref[C + C // 2 :, :] = jnp.broadcast_to(bias + pltpu.roll(bias, C, 1), (8, 128))


def meet_kernel(
    cols, fa_ref, x_ref, r_a, r_b, g_ref, u_part, part_ref, first_ref, u_ref, keep_ref, give_ref, cat, *, scale
):
    put_cat(cat, RIM, x_ref[...])
    for row, r in zip(rim_rows(cols), (r_a, r_b)):
        put_cat(cat, row, r[0:RIM, :])
        half = pl.ds(rim_half(row), RIM)
        u_ref[half, :] = u_part[half, :] + r[RIM : 2 * RIM, :]
    hop(cols, fa_ref, cat, first_ref, rim_block)
    g_rim = jnp.concatenate([g_ref[0:RIM, :], g_ref[ROWS - RIM :, :]], axis=0)
    ((one, two),) = products([first_ref[...]], [g_rim, u_ref[...]])
    total = part_ref[0 : 2 * HALF, :] + scale * packed(None, one, 2.0 * two)
    first = is_first_core(cols)
    keep_ref[0:HALF, :] = jnp.where(first, total[:HALF], total[HALF:])
    give_ref[0:HALF, :] = jnp.where(first, total[HALF:], total[:HALF])
    keep_ref[HALF:, :] = part_ref[2 * HALF :, :]
    give_ref[HALF:, :] = part_ref[2 * HALF :, :]


def inner_rows(g, u, w_ref):
    return mixed(g, both_maps(w_ref[1]).T) + 2.0 * mixed(u, both_maps(w_ref[2]).T)


def inner_mid_kernel(cols, at_ref, g_ref, u_ref, w_ref, acc, inner):
    inner[...] = inner_rows(g_ref[RIM : ROWS - RIM, :], u_ref[...], w_ref)
    acc[...] = jnp.zeros_like(acc)
    spread(cols, at_ref, inner, acc, mid_block)


def inner_rim_kernel(
    cols, at_ref, g_ref, u_ref, w_ref, first_ref, acc_in, u2_ref, send_a, send_b, inner, acc
):
    g_rim = jnp.concatenate([g_ref[0:RIM, :], g_ref[ROWS - RIM :, :]], axis=0)
    inner[...] = inner_rows(g_rim, u_ref[...], w_ref)
    acc[...] = acc_in[...]
    spread(cols, at_ref, inner, acc, rim_block)
    u2_ref[...] = acc[RIM : RIM + ROWS, :]
    for row, send in zip(rim_rows(cols), (send_a, send_b)):
        send[0:RIM, :] = first_ref[pl.ds(rim_half(row), RIM), :]
        send[RIM : 2 * RIM, :] = acc[pl.ds(row, RIM), :]


def outputs(x, g, one, hopped, w_ref, bias_ref):
    bias = bias_ref[...]
    out = (
        mixed(x, both_maps(w_ref[0]))
        + mixed(one, both_maps(w_ref[1]))
        + mixed(2.0 * hopped - x, both_maps(w_ref[2]))
        + jnp.concatenate([bias, bias], axis=1)
    )
    return out, mixed(g, both_maps(w_ref[0] - w_ref[2]).T)


def last_mid_kernel(
    cols, fa_ref, x_ref, g_ref, f_mid, f_rim, u2_ref, w_ref, bias_ref, out_ref, back_ref, cat, second
):
    put_cat(cat, RIM, f_rim[0:RIM, :])
    put_cat(cat, 2 * RIM, f_mid[...])
    put_cat(cat, 4 * RIM, f_rim[RIM : 2 * RIM, :])
    hop(cols, fa_ref, cat, second, mid_block)
    mid = slice(RIM, ROWS - RIM)
    out, back = outputs(x_ref[mid, :], g_ref[mid, :], f_mid[...], second[...], w_ref, bias_ref)
    out_ref[...] = out
    back_ref[...] = back + u2_ref[mid, :]


def last_rim_kernel(
    cols, fa_ref, x_ref, g_ref, f_mid, f_rim, r_a, r_b, u2_ref, w_ref, bias_ref, o_mid, b_mid,
    out_ref, back_ref, cat, second,
):
    put_cat(cat, RIM, f_rim[0:RIM, :])
    put_cat(cat, 2 * RIM, f_mid[...])
    put_cat(cat, 4 * RIM, f_rim[RIM : 2 * RIM, :])
    for row, r in zip(rim_rows(cols), (r_a, r_b)):
        put_cat(cat, row, r[0:RIM, :])
    hop(cols, fa_ref, cat, second, rim_block)
    x = jnp.concatenate([x_ref[0:RIM, :], x_ref[ROWS - RIM :, :]], axis=0)
    g = jnp.concatenate([g_ref[0:RIM, :], g_ref[ROWS - RIM :, :]], axis=0)
    out, back = outputs(x, g, f_rim[...], second[...], w_ref, bias_ref)
    mid = slice(RIM, ROWS - RIM)
    out_ref[mid, :] = o_mid[...]
    back_ref[mid, :] = b_mid[...]
    for at, half in ((0, 0), (ROWS - RIM, RIM)):
        out_ref[at : at + RIM, :] = out[half : half + RIM]
        back_ref[at : at + RIM, :] = back[half : half + RIM] + u2_ref[at : at + RIM, :]
    for row, r in zip(rim_rows(cols), (r_a, r_b)):
        own = pl.ds(pl.multiple_of(jnp.where(row == 0, 0, ROWS - RIM), RIM), RIM)
        back_ref[own, :] = back_ref[own, :] + r[RIM : 2 * RIM, :]


def final_kernel(cols, mine, theirs, weight_ref, bias_ref):
    first = is_first_core(cols)
    top = jnp.where(first, mine[...], theirs[...])
    bottom = jnp.where(first, theirs[...], mine[...])
    rest = C - HALF
    for k, (upper, lower) in enumerate(
        ((top, bottom), (pltpu.roll(top, C, 1), pltpu.roll(bottom, C, 1)))
    ):
        weight_ref[k, 0:HALF, :] = upper[:HALF, :C]
        weight_ref[k, HALF:C, :] = lower[:rest, :C]
        weight_ref[2, k * (C // 2) : (k + 1) * (C // 2), :] = lower[rest:HALF, :C]
    bias_ref[...] = top[HALF : HALF + 1, :C]


def call(kernel, out, specs, scratch, flops, moved):
    return pl.pallas_call(
        kernel,
        out_shape=[jax.ShapeDtypeStruct(s, d) for s, d in out],
        in_specs=specs,
        out_specs=[VMEM] * len(out),
        scratch_shapes=scratch,
        compiler_params=pltpu.CompilerParams(vmem_limit_bytes=24 * 1024 * 1024),
        cost_estimate=pl.CostEstimate(flops=flops, bytes_accessed=moved, transcendentals=0),
    )


def index(a, b, c, s):
    return ((a * SHAPE[1] + b) * SHAPE[2] + c) * SHAPE[3] + s


def place(i):
    return (i // 64, (i // 8) % 8, (i // 2) % 4, i % 2)


COUNT = 256
IN_CHIP = [(i, i ^ 1) for i in range(COUNT)]
CROSS = [(i, (i + 1) % COUNT) if i % 2 else (i, (i - 1) % COUNT) for i in range(COUNT)]
RING4 = ((1, 0, 3, 2), (3, 2, 1, 0))
PAIRS = (1, 0, 3, 2, 5, 4, 7, 6)
FAR = (5, 4, 7, 6, 1, 0, 3, 2)
NEXT = (6, 3, 0, 5, 2, 7, 4, 1)
NEAR = (7, 2, 1, 4, 3, 6, 5, 0)


def along(axis, table):
    pairs = []
    for i in range(COUNT):
        at = list(place(i))
        at[axis] = table[at[axis]]
        pairs.append((i, index(*at)))
    return pairs


def sent(value, pairs):
    return lax.ppermute(value, AXES, pairs)


def by_pair(own, near, following, far):
    z = lax.axis_index("patch_1")
    q, step = z // 2, 2 * (z % 2) - 1
    at = [jnp.bitwise_and(q + offset, 3) for offset in (0, step, -step, 2)]
    terms = []
    for k in range(4):
        term = far
        for place_of, value in zip(at[:3], (own, near, following)):
            term = jnp.where(place_of == k, value, term)
        terms.append(term)
    return (terms[0] + terms[1]) + (terms[2] + terms[3])


def shards(features, lap_tiles, columns, weights, bias_term, cotangent):
    scale = 1.0 / math.sqrt(BATCH * PB * BLOCKS)
    field = ((ROWS, W2), F32)
    half = ((ROWS // 2, W2), F32)
    extended = ((EXT * PB, W2), F32)
    sums = ((2 * HALF + 8, W2), F32)
    share = ((HALF + 8, W2), F32)
    natural = ((MID, 2 * PB, NB * PB), BF16)
    turned = ((MID, NB * PB, 2 * PB), BF16)
    raw = ((NB, BLK_DEV // 8, CHUNKS * 8, 128), F32)
    cat = pltpu.VMEM((EXT * PB, 2 * W2), BF16)
    half_scratch = pltpu.VMEM((ROWS // 2, W2), F32)

    def scaled(kernel):
        def body(*refs):
            kernel(*refs, scale=scale)

        return body

    in_hbm = [
        pltpu.with_memory_space_constraint(value, pltpu.HBM)
        for value in (columns.T, jnp.transpose(lap_tiles, (1, 0, 2)), cotangent, features)
    ]
    cols, raw, fa_rim, at_rim, acc, s_a, s_b = call(
        rim_kernel,
        [((NB, BLK_DEV), jnp.int32), raw, natural, turned, extended, half, half],
        [HBM] * 4,
        [
            pltpu.SMEM((NB, BLK_DEV), jnp.int32), half_scratch, half_scratch,
            pltpu.SemaphoreType.DMA((2 * CHUNKS,)), pltpu.SemaphoreType.DMA((6,)),
        ],
        400_000_000, 4_000_000,
    )(*in_hbm)
    r_b = sent(s_b, CROSS)
    r_a = sent(s_a, IN_CHIP)
    fa_mid, at_mid, f_mid, u_mid, u_rim, part = call(
        scaled(mid_kernel), [natural, turned, half, half, half, sums],
        [SMEM] + [VMEM] * 4, [cat, pltpu.VMEM(*extended)], 1_600_000_000, 9_000_000,
    )(cols, raw, cotangent, features, acc)
    f_rim, u_rim, keep, give = call(
        scaled(meet_kernel), [half, half, share, share], [SMEM] + [VMEM] * 7, [cat],
        400_000_000, 3_000_000,
    )(cols, fa_rim, features, r_a, r_b, cotangent, u_rim, part)
    grads = keep + sent(give, IN_CHIP)
    (acc,) = call(
        inner_mid_kernel, [extended], [SMEM] + [VMEM] * 4, [half_scratch],
        400_000_000, 3_000_000,
    )(cols, at_mid, cotangent, u_mid, weights)
    u2, s_a, s_b = call(
        inner_rim_kernel, [field, half, half], [SMEM] + [VMEM] * 6,
        [half_scratch, pltpu.VMEM(*extended)], 400_000_000, 3_000_000,
    )(cols, at_rim, cotangent, u_rim, weights, f_rim, acc)
    s_b = sent(s_b, CROSS)
    s_a = sent(s_a, IN_CHIP)
    bias_row = bias_term.reshape(1, C)
    o_mid, b_mid = call(
        last_mid_kernel, [half, half], [SMEM] + [VMEM] * 8, [cat, half_scratch],
        600_000_000, 4_000_000,
    )(cols, fa_mid, features, cotangent, f_mid, f_rim, u2, weights, bias_row)
    output, input_grad = call(
        last_rim_kernel, [field, field], [SMEM] + [VMEM] * 12, [cat, half_scratch],
        600_000_000, 5_000_000,
    )(cols, fa_rim, features, cotangent, f_mid, f_rim, s_a, s_b, u2, weights, bias_row, o_mid, b_mid)
    grads = grads + sent(grads, along(2, RING4[0]))
    grads = grads + sent(grads, along(2, RING4[1]))
    grads = grads + sent(grads, along(0, RING4[0]))
    grads = grads + sent(grads, along(0, RING4[1]))
    grads = grads + sent(grads, along(1, PAIRS))
    far = sent(grads, along(1, FAR))
    following = sent(grads, along(1, NEXT))
    near = sent(grads, along(1, NEAR))
    grads = by_pair(grads, near, following, far)
    theirs = sent(grads, IN_CHIP)
    weight_grad, bias_grad = call(
        final_kernel, [((3, C, C), F32), ((1, C), F32)], [SMEM, VMEM, VMEM], [],
        1000, 100_000,
    )(cols, grads, theirs)
    return output, input_grad, weight_grad, bias_grad.reshape(C)


def solution(mesh):
    grid = Mesh(mesh.devices.reshape(*SHAPE), AXES)
    placed = (P(AXES, None), P(AXES, None, None), P(AXES, None), P(), P(), P(AXES, None))

    return jax.shard_map(
        shards,
        mesh=grid,
        in_specs=placed,
        out_specs=(P(AXES, None), P(AXES, None), P(), P()),
        check_vma=False,
    )
```

```python
import math

import jax
import jax.numpy as jnp
from jax import lax
from jax.experimental import pallas as pl
from jax.experimental.pallas import tpu as pltpu
from jax.sharding import Mesh
from jax.sharding import PartitionSpec as P


C = 64
BATCH = 2
PB = 64
NB = 6
HB = 4
BLK_DEV = 16
ROWS = BLK_DEV * PB
RIM = HB * PB
EXT = BLK_DEV + 2 * HB
MID = BLK_DEV - 2 * HB
HALF = 3 * C // 4
W2 = BATCH * C
CHUNKS = PB * PB // 128
AXES = ("patch_0", "patch_1", "patch_2", "strip")
SHAPE = (4, 8, 4, 2)
BLOCKS = 4096
F32 = jnp.float32
BF16 = jnp.bfloat16
VMEM = pl.BlockSpec(memory_space=pltpu.VMEM)
SMEM = pl.BlockSpec(memory_space=pltpu.SMEM)
HBM = pl.BlockSpec(memory_space=pltpu.HBM)


def split(value):
    high = value.astype(BF16)
    return high, (value - high.astype(F32)).astype(BF16)


def mm(a, b):
    return jnp.dot(a, b, preferred_element_type=F32)


def mm_tn(a, b):
    return lax.dot_general(a, b, (((0,), (0,)), ((), ())), preferred_element_type=F32)


def slot_of(cols, b, j):
    return jnp.bitwise_and(cols[j, b] - cols[0, 0] + HB, BLOCKS - 1)


def is_first_core(cols):
    return jnp.bitwise_and(cols[0, 0] // BLK_DEV, 1) == 0


def rim_rows(cols):
    first = is_first_core(cols)
    low, high = 0, (BLK_DEV + HB) * PB
    return (
        pl.multiple_of(jnp.where(first, high, low), RIM),
        pl.multiple_of(jnp.where(first, low, high), RIM),
    )


def rim_half(row):
    return pl.multiple_of(jnp.where(row == 0, 0, RIM), RIM)


def rim_block(i):
    return jnp.where(i < HB, i, i + MID)


def mid_block(i):
    return i + HB


def block_rows(ref, i):
    return jnp.concatenate(
        [ref[pl.ds(i * PB, PB // 2, stride=2), :], ref[pl.ds(i * PB + 1, PB // 2, stride=2), :]],
        axis=0,
    )


def rows_of(slot):
    return pl.ds(pl.multiple_of(slot * PB, PB), PB)


def spread(cols, at_ref, vec_ref, acc, block):
    def one(i, carry):
        b = block(i)
        high, low = split(block_rows(vec_ref, i))
        rhs = jnp.concatenate([high, high, low, low], axis=0)
        at = at_ref[i]
        out = mm(jnp.concatenate([at, at], axis=1), rhs)
        for j in range(NB):
            rows = rows_of(slot_of(cols, b, j))
            acc[rows, :] = acc[rows, :] + out[j * PB : (j + 1) * PB]
        return carry

    lax.fori_loop(0, MID, one, 0, unroll=8)


def hop(cols, fa_ref, cat, out_ref, block):
    def one(i, carry):
        b = block(i)
        rhs = jnp.concatenate([cat[rows_of(slot_of(cols, b, j)), :] for j in range(NB)], axis=0)
        out = mm(fa_ref[i], rhs)
        out = out[:, :W2] + out[:, W2:]
        out = out[:PB] + out[PB:]
        out_ref[pl.ds(i * PB, PB // 2, stride=2), :] = out[: PB // 2]
        out_ref[pl.ds(i * PB + 1, PB // 2, stride=2), :] = out[PB // 2 :]
        return carry

    lax.fori_loop(0, MID, one, 0, unroll=8)


def put_cat(cat, start, value):
    high, low = split(value)
    cat[pl.ds(start, value.shape[0]), :] = jnp.concatenate([high, low], axis=1)


def build(raw, fa_ref, at_ref, block, start=0, stop=MID):
    low_lanes = lax.broadcasted_iota(jnp.int32, (CHUNKS, 128), 1) < PB

    def one(i, carry):
        b = block(i)
        group, rows = b // 8, pl.ds(b % 8, CHUNKS, stride=8)
        for pair in range(NB // 2):
            even = raw[2 * pair, group, rows, :]
            odd = raw[2 * pair + 1, group, rows, :]
            top = jnp.where(low_lanes, even, pltpu.roll(odd, PB, 1))
            bottom = jnp.where(low_lanes, pltpu.roll(even, PB, 1), odd)
            both = jnp.concatenate([top, bottom], axis=0)
            high = both.astype(BF16)
            low = (both - high.astype(F32)).astype(BF16)
            lanes = pl.ds(pair * 128, 128)
            stacked = jnp.concatenate([high, low], axis=0)
            fa_ref[i, :, lanes] = stacked
            at_ref[i, lanes, :] = stacked.T
        return carry

    lax.fori_loop(start, stop, one, 0, unroll=4)


def rim_kernel(
    cols_hbm, tiles, g_hbm, x_hbm,
    cols_ref, raw, fa_ref, at_ref, acc, send_a, send_b,
    cols, g_rim, x_rim, sem, small,
):
    to_cols = pltpu.make_async_copy(cols_hbm, cols, small.at[0])
    others = [pltpu.make_async_copy(cols_hbm, cols_ref, small.at[1])]
    for n, (value, to) in enumerate(((g_hbm, g_rim), (x_hbm, x_rim))):
        others.append(
            pltpu.make_async_copy(value.at[pl.ds(0, RIM)], to.at[pl.ds(0, RIM)], small.at[2 + 2 * n])
        )
        others.append(
            pltpu.make_async_copy(
                value.at[pl.ds(ROWS - RIM, RIM)], to.at[pl.ds(RIM, RIM)], small.at[3 + 2 * n]
            )
        )
    copies = [
        pltpu.make_async_copy(
            tiles.at[:, pl.ds(8 * group, 8), pl.ds(k * 128, 128)],
            raw.at[:, group, pl.ds(8 * k, 8), :],
            sem.at[group * CHUNKS + k],
        )
        for group in range(BLK_DEV // 8)
        for k in range(CHUNKS)
    ]
    for copy in copies + [to_cols] + others:
        copy.start()
    acc[...] = jnp.zeros_like(acc)
    for copy in copies[:CHUNKS]:
        copy.wait()
    build(raw, fa_ref, at_ref, rim_block, 0, HB)
    for copy in copies[CHUNKS:]:
        copy.wait()
    build(raw, fa_ref, at_ref, rim_block, HB, MID)
    to_cols.wait()
    for copy in others:
        copy.wait()
    spread(cols, at_ref, g_rim, acc, rim_block)
    for row, send in zip(rim_rows(cols), (send_a, send_b)):
        send[0:RIM, :] = x_rim[pl.ds(rim_half(row), RIM), :]
        send[RIM : 2 * RIM, :] = acc[pl.ds(row, RIM), :]


def maps_sum(full):
    return full[:C] + pltpu.roll(full[C:], C, 1)


def products(left, right):
    a = jnp.concatenate([h for value in left for h in split(value)], axis=1)
    b = jnp.concatenate([h for value in right for h in split(value)], axis=1)
    out = mm_tn(a, b)
    result = []
    for p in range(len(left)):
        band = out[2 * p * W2 : (2 * p + 1) * W2] + out[(2 * p + 1) * W2 : (2 * p + 2) * W2]
        result.append(
            [
                band[:, 2 * q * W2 : (2 * q + 1) * W2] + band[:, (2 * q + 1) * W2 : (2 * q + 2) * W2]
                for q in range(len(right))
            ]
        )
    return result


def packed(zero, one, two):
    low_lanes = lax.broadcasted_iota(jnp.int32, (C, 128), 1) < C
    two = maps_sum(two)
    one = pltpu.roll(maps_sum(one), C, 1)
    if zero is None:
        top = jnp.where(low_lanes, 0.0, one)
    else:
        top = jnp.where(low_lanes, maps_sum(zero), one)
    bottom = jnp.where(low_lanes[: C // 2], two[: C // 2], pltpu.roll(two[C // 2 :], C, 1))
    return jnp.concatenate([top, bottom], axis=0)


def both_maps(weight):
    zero = jnp.zeros_like(weight)
    return jnp.concatenate(
        [jnp.concatenate([weight, zero], axis=1), jnp.concatenate([zero, weight], axis=1)], axis=0
    )


def mixed(value, weight):
    high, low = split(value)
    w_high, w_low = split(weight)
    row = jnp.concatenate([w_high, w_low], axis=1)
    out = mm(jnp.concatenate([high, low], axis=1), jnp.concatenate([row, row], axis=0))
    return out[:, :W2] + out[:, W2:]


def mid_kernel(
    cols, raw, g_ref, x_ref, acc_in,
    fa_ref, at_ref, first_ref, u_mid, u_rim, part_ref, cat,
    acc, *, scale,
):
    put_cat(cat, RIM, x_ref[...])
    acc[...] = acc_in[...]
    build(raw, fa_ref, at_ref, mid_block)
    g_mid = g_ref.at[pl.ds(RIM, MID * PB)]
    spread(cols, at_ref, g_mid, acc, mid_block)
    u_mid[...] = acc[2 * RIM : 4 * RIM, :]
    u_rim[0:RIM, :] = acc[RIM : 2 * RIM, :]
    u_rim[RIM : 2 * RIM, :] = acc[4 * RIM : 5 * RIM, :]
    hop(cols, fa_ref, cat, first_ref, mid_block)
    ((zero,),) = products([x_ref[...]], [g_ref[...]])
    ((one, two),) = products([first_ref[...]], [g_mid[...], u_mid[...]])
    part_ref[0 : C + C // 2, :] = scale * packed(zero, one, 2.0 * two - zero)
    bias = scale * jnp.sum(g_ref[...], axis=0, keepdims=True)
    part_ref[C + C // 2 :, :] = jnp.broadcast_to(bias + pltpu.roll(bias, C, 1), (8, 128))


def meet_kernel(
    cols, fa_ref, cat_in, r_a, r_b, g_ref, u_part, part_ref,
    first_ref, u_ref, keep_ref, give_ref, cat, *, scale
):
    del cat_in
    for row, r in zip(rim_rows(cols), (r_a, r_b)):
        put_cat(cat, row, r[0:RIM, :])
        half = pl.ds(rim_half(row), RIM)
        u_ref[half, :] = u_part[half, :] + r[RIM : 2 * RIM, :]
    hop(cols, fa_ref, cat, first_ref, rim_block)
    g_rim = jnp.concatenate([g_ref[0:RIM, :], g_ref[ROWS - RIM :, :]], axis=0)
    ((one, two),) = products([first_ref[...]], [g_rim, u_ref[...]])
    total = part_ref[0 : 2 * HALF, :] + scale * packed(None, one, 2.0 * two)
    first = is_first_core(cols)
    keep_ref[0:HALF, :] = jnp.where(first, total[:HALF], total[HALF:])
    give_ref[0:HALF, :] = jnp.where(first, total[HALF:], total[:HALF])
    keep_ref[HALF:, :] = part_ref[2 * HALF :, :]
    give_ref[HALF:, :] = part_ref[2 * HALF :, :]


def inner_rows(g, u, w_ref):
    return mixed(g, both_maps(w_ref[1]).T) + 2.0 * mixed(u, both_maps(w_ref[2]).T)


def inner_mid_kernel(cols, at_ref, g_ref, u_ref, w_ref, acc, inner):
    inner[...] = inner_rows(g_ref[RIM : ROWS - RIM, :], u_ref[...], w_ref)
    acc[...] = jnp.zeros_like(acc)
    spread(cols, at_ref, inner, acc, mid_block)


def inner_rim_kernel(
    cols, at_ref, g_ref, u_ref, w_ref, first_ref, acc_in, u2_ref, send_a, send_b, inner, acc
):
    g_rim = jnp.concatenate([g_ref[0:RIM, :], g_ref[ROWS - RIM :, :]], axis=0)
    inner[...] = inner_rows(g_rim, u_ref[...], w_ref)
    acc[...] = acc_in[...]
    spread(cols, at_ref, inner, acc, rim_block)
    u2_ref[...] = acc[RIM : RIM + ROWS, :]
    for row, send in zip(rim_rows(cols), (send_a, send_b)):
        send[0:RIM, :] = first_ref[pl.ds(rim_half(row), RIM), :]
        send[RIM : 2 * RIM, :] = acc[pl.ds(row, RIM), :]


def outputs(x, g, one, hopped, w_ref, bias_ref):
    bias = bias_ref[...]
    out = (
        mixed(x, both_maps(w_ref[0]))
        + mixed(one, both_maps(w_ref[1]))
        + mixed(2.0 * hopped - x, both_maps(w_ref[2]))
        + jnp.concatenate([bias, bias], axis=1)
    )
    return out, mixed(g, both_maps(w_ref[0] - w_ref[2]).T)


def own_cat(cat, f_mid, f_rim):
    put_cat(cat, RIM, f_rim[0:RIM, :])
    put_cat(cat, 2 * RIM, f_mid[...])
    put_cat(cat, 4 * RIM, f_rim[RIM : 2 * RIM, :])


def last_mid_kernel(
    cols, fa_ref, x_ref, g_ref, f_mid, f_rim, u2_ref, w_ref, bias_ref,
    out_hbm, back_hbm, cat, second, out_ref, back_ref, sem,
):
    own_cat(cat, f_mid, f_rim)
    hop(cols, fa_ref, cat, second, mid_block)
    mid = slice(RIM, ROWS - RIM)
    out, back = outputs(x_ref[mid, :], g_ref[mid, :], f_mid[...], second[...], w_ref, bias_ref)
    out_ref[...] = out
    back_ref[...] = back + u2_ref[mid, :]
    copies = [
        pltpu.make_async_copy(value, to.at[pl.ds(RIM, MID * PB)], sem.at[n])
        for n, (value, to) in enumerate(((out_ref, out_hbm), (back_ref, back_hbm)))
    ]
    for copy in copies:
        copy.start()
    for copy in copies:
        copy.wait()


def last_rim_kernel(
    cols, fa_ref, x_ref, g_ref, f_mid, f_rim, r_a, r_b, u2_ref, w_ref, bias_ref, o_in, b_in,
    out_hbm, back_hbm, cat, second, out_ref, back_ref, sem,
):
    del o_in, b_in
    own_cat(cat, f_mid, f_rim)
    for row, r in zip(rim_rows(cols), (r_a, r_b)):
        put_cat(cat, row, r[0:RIM, :])
    hop(cols, fa_ref, cat, second, rim_block)
    x = jnp.concatenate([x_ref[0:RIM, :], x_ref[ROWS - RIM :, :]], axis=0)
    g = jnp.concatenate([g_ref[0:RIM, :], g_ref[ROWS - RIM :, :]], axis=0)
    out, back = outputs(x, g, f_rim[...], second[...], w_ref, bias_ref)
    out_ref[...] = out
    back_ref[...] = back + jnp.concatenate([u2_ref[0:RIM, :], u2_ref[ROWS - RIM :, :]], axis=0)
    for row, r in zip(rim_rows(cols), (r_a, r_b)):
        half = pl.ds(rim_half(row), RIM)
        back_ref[half, :] = back_ref[half, :] + r[RIM : 2 * RIM, :]
    copies = [
        pltpu.make_async_copy(
            value.at[pl.ds(n * RIM, RIM)], to.at[pl.ds(n * (ROWS - RIM), RIM)], sem.at[2 * k + n]
        )
        for k, (value, to) in enumerate(((out_ref, out_hbm), (back_ref, back_hbm)))
        for n in range(2)
    ]
    for copy in copies:
        copy.start()
    for copy in copies:
        copy.wait()


def pairs_kernel(cols, own, near, following, far, total_ref):
    place = cols[0:1, 0:1] // BLK_DEV
    z = jnp.bitwise_and(place // 8, 7)
    q, step = z // 2, 2 * jnp.bitwise_and(z, 1) - 1
    at = [jnp.bitwise_and(q + offset, 3) for offset in (0, step, -step)]
    terms = []
    for k in range(4):
        term = far[...]
        for source, value in zip(at, (own, near, following)):
            term = jnp.where(jnp.broadcast_to(source, term.shape) == k, value[...], term)
        terms.append(term)
    total_ref[...] = (terms[0] + terms[1]) + (terms[2] + terms[3])


def final_kernel(cols, mine, theirs, weight_ref, bias_ref):
    core = jnp.bitwise_and(cols[0:1, 0:1] // BLK_DEV, 1)
    first = jnp.broadcast_to(core, mine.shape) == 0
    top = jnp.where(first, mine[...], theirs[...])
    bottom = jnp.where(first, theirs[...], mine[...])
    rest = C - HALF
    for k, (upper, lower) in enumerate(
        ((top, bottom), (pltpu.roll(top, C, 1), pltpu.roll(bottom, C, 1)))
    ):
        weight_ref[k, 0:HALF, :] = upper[:HALF, :C]
        weight_ref[k, HALF:C, :] = lower[:rest, :C]
        weight_ref[2, k * (C // 2) : (k + 1) * (C // 2), :] = lower[rest:HALF, :C]
    bias_ref[...] = top[HALF : HALF + 1, :C]


def call(kernel, out, specs, scratch, flops, moved, places=None, aliases=None):
    return pl.pallas_call(
        kernel,
        out_shape=[jax.ShapeDtypeStruct(s, d) for s, d in out],
        in_specs=specs,
        out_specs=places or [VMEM] * len(out),
        input_output_aliases=aliases or {},
        scratch_shapes=scratch,
        compiler_params=pltpu.CompilerParams(vmem_limit_bytes=24 * 1024 * 1024),
        cost_estimate=pl.CostEstimate(flops=flops, bytes_accessed=moved, transcendentals=0),
    )


def index(a, b, c, s):
    return ((a * SHAPE[1] + b) * SHAPE[2] + c) * SHAPE[3] + s


def place(i):
    return (i // 64, (i // 8) % 8, (i // 2) % 4, i % 2)


COUNT = 256
IN_CHIP = [(i, i ^ 1) for i in range(COUNT)]
CROSS = [(i, (i + 1) % COUNT) if i % 2 else (i, (i - 1) % COUNT) for i in range(COUNT)]
RING4 = ((1, 0, 3, 2), (3, 2, 1, 0))
PAIRS = (1, 0, 3, 2, 5, 4, 7, 6)
FAR = (5, 4, 7, 6, 1, 0, 3, 2)
NEXT = (6, 3, 0, 5, 2, 7, 4, 1)
NEAR = (7, 2, 1, 4, 3, 6, 5, 0)


def along(axis, table):
    pairs = []
    for i in range(COUNT):
        at = list(place(i))
        at[axis] = table[at[axis]]
        pairs.append((i, index(*at)))
    return pairs


def sent(value, pairs):
    return lax.ppermute(value, AXES, pairs)


def shards(features, lap_tiles, columns, weights, bias_term, cotangent):
    scale = 1.0 / math.sqrt(BATCH * PB * BLOCKS)
    field = ((ROWS, W2), F32)
    half = ((ROWS // 2, W2), F32)
    extended = ((EXT * PB, W2), F32)
    sums = ((2 * HALF + 8, W2), F32)
    share = ((HALF + 8, W2), F32)
    natural = ((MID, 2 * PB, NB * PB), BF16)
    turned = ((MID, NB * PB, 2 * PB), BF16)
    raw = ((NB, BLK_DEV // 8, CHUNKS * 8, 128), F32)
    cat = pltpu.VMEM((EXT * PB, 2 * W2), BF16)
    half_scratch = pltpu.VMEM((ROWS // 2, W2), F32)

    def scaled(kernel):
        def body(*refs):
            kernel(*refs, scale=scale)

        return body

    in_hbm = [
        pltpu.with_memory_space_constraint(value, pltpu.HBM)
        for value in (columns.T, jnp.transpose(lap_tiles, (1, 0, 2)), cotangent, features)
    ]
    cols, raw, fa_rim, at_rim, acc, s_a, s_b = call(
        rim_kernel,
        [((NB, BLK_DEV), jnp.int32), raw, natural, turned, extended, half, half],
        [HBM] * 4,
        [
            pltpu.SMEM((NB, BLK_DEV), jnp.int32), half_scratch, half_scratch,
            pltpu.SemaphoreType.DMA((2 * CHUNKS,)), pltpu.SemaphoreType.DMA((6,)),
        ],
        400_000_000, 4_000_000,
    )(*in_hbm)
    r_b = sent(s_b, CROSS)
    r_a = sent(s_a, IN_CHIP)
    catted = ((EXT * PB, 2 * W2), BF16)
    fa_mid, at_mid, f_mid, u_mid, u_rim, part, own_x = call(
        scaled(mid_kernel), [natural, turned, half, half, half, sums, catted],
        [SMEM] + [VMEM] * 4, [pltpu.VMEM(*extended)], 1_600_000_000, 9_000_000,
    )(cols, raw, cotangent, features, acc)
    f_rim, u_rim, keep, give, _ = call(
        scaled(meet_kernel), [half, half, share, share, catted], [SMEM] + [VMEM] * 7, [],
        400_000_000, 3_000_000, aliases={2: 4},
    )(cols, fa_rim, own_x, r_a, r_b, cotangent, u_rim, part)
    grads = keep + sent(give, IN_CHIP)
    (acc,) = call(
        inner_mid_kernel, [extended], [SMEM] + [VMEM] * 4, [half_scratch],
        400_000_000, 3_000_000,
    )(cols, at_mid, cotangent, u_mid, weights)
    u2, s_a, s_b = call(
        inner_rim_kernel, [field, half, half], [SMEM] + [VMEM] * 6,
        [half_scratch, pltpu.VMEM(*extended)], 400_000_000, 3_000_000,
    )(cols, at_rim, cotangent, u_rim, weights, f_rim, acc)
    s_b = sent(s_b, CROSS)
    s_a = sent(s_a, IN_CHIP)
    bias_row = bias_term.reshape(1, C)
    scratch = [cat, half_scratch, half_scratch, half_scratch]
    output, input_grad = call(
        last_mid_kernel, [field, field], [SMEM] + [VMEM] * 8,
        scratch + [pltpu.SemaphoreType.DMA((2,))], 600_000_000, 4_000_000, places=[HBM, HBM],
    )(cols, fa_mid, features, cotangent, f_mid, f_rim, u2, weights, bias_row)
    output, input_grad = call(
        last_rim_kernel, [field, field], [SMEM] + [VMEM] * 10 + [HBM, HBM],
        scratch + [pltpu.SemaphoreType.DMA((4,))], 600_000_000, 5_000_000,
        places=[HBM, HBM], aliases={11: 0, 12: 1},
    )(
        cols, fa_rim, features, cotangent, f_mid, f_rim, s_a, s_b, u2, weights, bias_row,
        output, input_grad,
    )
    grads = grads + sent(grads, along(2, RING4[0]))
    grads = grads + sent(grads, along(2, RING4[1]))
    grads = grads + sent(grads, along(0, RING4[0]))
    grads = grads + sent(grads, along(0, RING4[1]))
    grads = grads + sent(grads, along(1, PAIRS))
    far = sent(grads, along(1, FAR))
    following = sent(grads, along(1, NEXT))
    near = sent(grads, along(1, NEAR))
    (grads,) = call(pairs_kernel, [share], [VMEM] * 5, [], 1000, 100_000)(
        cols, grads, near, following, far
    )
    theirs = sent(grads, IN_CHIP)
    weight_grad, bias_grad = call(
        final_kernel, [((3, C, C), F32), ((1, C), F32)], [VMEM] * 3, [],
        1000, 100_000,
    )(cols, grads, theirs)
    return output, input_grad, weight_grad, bias_grad.reshape(C)


def solution(mesh):
    grid = Mesh(mesh.devices.reshape(*SHAPE), AXES)
    placed = (P(AXES, None), P(AXES, None, None), P(AXES, None), P(), P(), P(AXES, None))

    return jax.shard_map(
        shards,
        mesh=grid,
        in_specs=placed,
        out_specs=(P(AXES, None), P(AXES, None), P(), P()),
        check_vma=False,
    )
```

```python
import math

import jax
import jax.numpy as jnp
from jax import lax
from jax.experimental import pallas as pl
from jax.experimental.pallas import tpu as pltpu
from jax.sharding import Mesh
from jax.sharding import PartitionSpec as P


C = 64
BATCH = 2
PB = 64
NB = 6
HB = 4
BLK_DEV = 16
ROWS = BLK_DEV * PB
RIM = HB * PB
EXT = BLK_DEV + 2 * HB
MID = BLK_DEV - 2 * HB
HALF = 3 * C // 4
W2 = BATCH * C
CHUNKS = PB * PB // 128
AXES = ("patch_0", "patch_1", "patch_2", "strip")
SHAPE = (4, 8, 4, 2)
BLOCKS = 4096
F32 = jnp.float32
BF16 = jnp.bfloat16
VMEM = pl.BlockSpec(memory_space=pltpu.VMEM)
SMEM = pl.BlockSpec(memory_space=pltpu.SMEM)
HBM = pl.BlockSpec(memory_space=pltpu.HBM)


def split(value):
    high = value.astype(BF16)
    return high, (value - high.astype(F32)).astype(BF16)


def mm(a, b):
    return jnp.dot(a, b, preferred_element_type=F32)


def mm_tn(a, b):
    return lax.dot_general(a, b, (((0,), (0,)), ((), ())), preferred_element_type=F32)


def slot_of(cols, b, j):
    return jnp.bitwise_and(cols[j, b] - cols[0, 0] + HB, BLOCKS - 1)


def strip_of(cols):
    return jnp.bitwise_and(cols[0, 0] // BLK_DEV, 1)


class Side:
    def __init__(self, end):
        self.own = pl.multiple_of(end * (ROWS - RIM), RIM)
        self.slots = pl.multiple_of(self.own + RIM, RIM)
        self.beyond = pl.multiple_of(end * ((BLK_DEV + HB) * PB), RIM)
        self.half = pl.multiple_of(end * RIM, RIM)
        self.first = end * (BLK_DEV - HB)

    def block(self, i):
        return self.first + i


def both_sides(cols):
    strip = strip_of(cols)
    return Side(strip), Side(1 - strip)


def mid_block(i):
    return i + HB


def block_rows(ref, at):
    return jnp.concatenate(
        [ref[pl.ds(at, PB // 2, stride=2), :], ref[pl.ds(at + 1, PB // 2, stride=2), :]], axis=0
    )


def rows_of(slot):
    return pl.ds(pl.multiple_of(slot * PB, PB), PB)


def spread(cols, at_ref, vec_ref, acc, block, count=MID, start=0):
    def one(i, carry):
        b = block(i)
        high, low = split(block_rows(vec_ref, start + i * PB))
        rhs = jnp.concatenate([high, high, low, low], axis=0)
        at = at_ref[i]
        out = mm(jnp.concatenate([at, at], axis=1), rhs)
        for j in range(NB):
            rows = rows_of(slot_of(cols, b, j))
            acc[rows, :] = acc[rows, :] + out[j * PB : (j + 1) * PB]
        return carry

    lax.fori_loop(0, count, one, 0, unroll=count)


def hop(cols, fa_ref, cat, out_ref, block, count=MID, start=0):
    def one(i, carry):
        b = block(i)
        rhs = jnp.concatenate([cat[rows_of(slot_of(cols, b, j)), :] for j in range(NB)], axis=0)
        out = mm(fa_ref[i], rhs)
        out = out[:, :W2] + out[:, W2:]
        out = out[:PB] + out[PB:]
        out_ref[pl.ds(start + i * PB, PB // 2, stride=2), :] = out[: PB // 2]
        out_ref[pl.ds(start + i * PB + 1, PB // 2, stride=2), :] = out[PB // 2 :]
        return carry

    lax.fori_loop(0, count, one, 0, unroll=count)


def put_cat(cat, start, value):
    high, low = split(value)
    cat[pl.ds(start, value.shape[0]), :] = jnp.concatenate([high, low], axis=1)


def build(raw, fa_ref, at_ref, block, count=MID):
    low_lanes = lax.broadcasted_iota(jnp.int32, (CHUNKS, 128), 1) < PB

    def one(i, carry):
        b = block(i)
        group, rows = b // 8, pl.ds(b % 8, CHUNKS, stride=8)
        for pair in range(NB // 2):
            even = raw[2 * pair, group, rows, :]
            odd = raw[2 * pair + 1, group, rows, :]
            top = jnp.where(low_lanes, even, pltpu.roll(odd, PB, 1))
            bottom = jnp.where(low_lanes, pltpu.roll(even, PB, 1), odd)
            both = jnp.concatenate([top, bottom], axis=0)
            high = both.astype(BF16)
            low = (both - high.astype(F32)).astype(BF16)
            lanes = pl.ds(pair * 128, 128)
            stacked = jnp.concatenate([high, low], axis=0)
            fa_ref[i, :, lanes] = stacked
            at_ref[i, lanes, :] = stacked.T
        return carry

    lax.fori_loop(0, count, one, 0, unroll=4)


def far_kernel(
    cols_hbm, tiles, g_hbm, x_hbm,
    cols_ref, raw, fa_ref, at_ref, acc, send,
    cols, g_rim, sem, small,
):
    strip = lax.axis_index("strip")
    side = Side(strip)

    def group_copies(group, n):
        return [
            pltpu.make_async_copy(
                tiles.at[:, pl.ds(pl.multiple_of(8 * group, 8), 8), pl.ds(k * 128, 128)],
                raw.at[:, group, pl.ds(8 * k, 8), :],
                sem.at[n * CHUNKS + k],
            )
            for k in range(CHUNKS)
        ]

    now, later = group_copies(strip, 0), group_copies(1 - strip, 1)
    rows = pl.ds(side.own, RIM)
    soon = [
        pltpu.make_async_copy(cols_hbm, cols, small.at[0]),
        pltpu.make_async_copy(g_hbm.at[rows], g_rim, small.at[1]),
    ]
    late = [
        pltpu.make_async_copy(cols_hbm, cols_ref, small.at[2]),
        pltpu.make_async_copy(x_hbm.at[rows], send.at[pl.ds(0, RIM)], small.at[3]),
    ]
    for copy in now + soon + late + later:
        copy.start()
    acc[...] = jnp.zeros_like(acc)
    for copy in now:
        copy.wait()
    build(raw, fa_ref, at_ref, side.block, HB)
    for copy in soon:
        copy.wait()
    spread(cols, at_ref, g_rim, acc, side.block, HB)
    send[RIM : 2 * RIM, :] = acc[pl.ds(side.beyond, RIM), :]
    for copy in late + later:
        copy.wait()


def near_kernel(cols, raw, g_ref, x_ref, acc_in, fa_ref, at_ref, acc, send):
    del acc_in
    _, side = both_sides(cols)
    build(raw, fa_ref, at_ref, side.block, HB)
    spread(cols, at_ref, g_ref, acc, side.block, HB, side.own)
    send[0:RIM, :] = x_ref[pl.ds(side.own, RIM), :]
    send[RIM : 2 * RIM, :] = acc[pl.ds(side.beyond, RIM), :]


def maps_sum(full):
    return full[:C] + pltpu.roll(full[C:], C, 1)


def products(left, right):
    a = jnp.concatenate([h for value in left for h in split(value)], axis=1)
    b = jnp.concatenate([h for value in right for h in split(value)], axis=1)
    out = mm_tn(a, b)
    result = []
    for p in range(len(left)):
        band = out[2 * p * W2 : (2 * p + 1) * W2] + out[(2 * p + 1) * W2 : (2 * p + 2) * W2]
        result.append(
            [
                band[:, 2 * q * W2 : (2 * q + 1) * W2] + band[:, (2 * q + 1) * W2 : (2 * q + 2) * W2]
                for q in range(len(right))
            ]
        )
    return result


def packed(zero, one, two):
    low_lanes = lax.broadcasted_iota(jnp.int32, (C, 128), 1) < C
    two = maps_sum(two)
    one = pltpu.roll(maps_sum(one), C, 1)
    if zero is None:
        top = jnp.where(low_lanes, 0.0, one)
    else:
        top = jnp.where(low_lanes, maps_sum(zero), one)
    bottom = jnp.where(low_lanes[: C // 2], two[: C // 2], pltpu.roll(two[C // 2 :], C, 1))
    return jnp.concatenate([top, bottom], axis=0)


def both_maps(weight):
    zero = jnp.zeros_like(weight)
    return jnp.concatenate(
        [jnp.concatenate([weight, zero], axis=1), jnp.concatenate([zero, weight], axis=1)], axis=0
    )


def mixed(value, weight):
    high, low = split(value)
    w_high, w_low = split(weight)
    row = jnp.concatenate([w_high, w_low], axis=1)
    out = mm(jnp.concatenate([high, low], axis=1), jnp.concatenate([row, row], axis=0))
    return out[:, :W2] + out[:, W2:]


def mid_kernel(
    cols, raw, g_ref, x_ref, acc_in,
    fa_ref, at_ref, first_ref, u_mid, u_b, u_a, part_ref, cat,
    acc, *, scale,
):
    put_cat(cat, RIM, x_ref[...])
    acc[...] = acc_in[...]
    build(raw, fa_ref, at_ref, mid_block)
    g_mid = g_ref.at[pl.ds(RIM, MID * PB)]
    spread(cols, at_ref, g_mid, acc, mid_block)
    u_mid[...] = acc[2 * RIM : 4 * RIM, :]
    for side, u in zip(both_sides(cols), (u_b, u_a)):
        u[...] = acc[pl.ds(side.slots, RIM), :]
    hop(cols, fa_ref, cat, first_ref, mid_block)
    ((zero,),) = products([x_ref[...]], [g_ref[...]])
    ((one, two),) = products([first_ref[...]], [g_mid[...], u_mid[...]])
    part_ref[0 : C + C // 2, :] = scale * packed(zero, one, 2.0 * two - zero)
    bias = scale * jnp.sum(g_ref[...], axis=0, keepdims=True)
    part_ref[C + C // 2 :, :] = jnp.broadcast_to(bias + pltpu.roll(bias, C, 1), (8, 128))


def side_rows(ref, sides):
    return jnp.concatenate([ref[pl.ds(side.own, RIM), :] for side in sides], axis=0)


def meet_kernel(
    cols, fa_b, fa_a, cat_in, r_b, r_a, g_ref, p_b, p_a, part_ref,
    f_b, f_a, u_b, u_a, keep_ref, give_ref, cat, *, scale
):
    del cat_in
    sides = both_sides(cols)
    for side, r, p, u in zip(sides, (r_b, r_a), (p_b, p_a), (u_b, u_a)):
        put_cat(cat, side.beyond, r[0:RIM, :])
        u[...] = p[...] + r[RIM : 2 * RIM, :]
    for side, fa_ref, first in zip(sides, (fa_b, fa_a), (f_b, f_a)):
        hop(cols, fa_ref, cat, first, side.block, HB)
    first = jnp.concatenate([f_b[...], f_a[...]], axis=0)
    u = jnp.concatenate([u_b[...], u_a[...]], axis=0)
    ((one, two),) = products([first], [side_rows(g_ref, sides), u])
    total = part_ref[0 : 2 * HALF, :] + scale * packed(None, one, 2.0 * two)
    lower = strip_of(cols) == 0
    keep_ref[0:HALF, :] = jnp.where(lower, total[:HALF], total[HALF:])
    give_ref[0:HALF, :] = jnp.where(lower, total[HALF:], total[:HALF])
    keep_ref[HALF:, :] = part_ref[2 * HALF :, :]
    give_ref[HALF:, :] = part_ref[2 * HALF :, :]


def inner_rows(g, u, w_ref):
    return mixed(g, both_maps(w_ref[1]).T) + 2.0 * mixed(u, both_maps(w_ref[2]).T)


def inner_mid_kernel(cols, at_ref, g_ref, u_ref, w_ref, acc, inner):
    inner[...] = inner_rows(g_ref[RIM : ROWS - RIM, :], u_ref[...], w_ref)
    acc[...] = jnp.zeros_like(acc)
    spread(cols, at_ref, inner, acc, mid_block)


def inner_rim_kernel(
    cols, at_b, at_a, g_ref, u_b, u_a, w_ref, f_b, f_a, acc_in,
    u2_ref, send_b, send_a, acc, inner,
):
    del acc_in
    sides = both_sides(cols)
    u = jnp.concatenate([u_b[...], u_a[...]], axis=0)
    inner[...] = inner_rows(side_rows(g_ref, sides), u, w_ref)
    for n, (side, at_ref) in enumerate(zip(sides, (at_b, at_a))):
        spread(cols, at_ref, inner, acc, side.block, HB, n * RIM)
    u2_ref[...] = acc[RIM : RIM + ROWS, :]
    for side, first, send in zip(sides, (f_b, f_a), (send_b, send_a)):
        send[0:RIM, :] = first[...]
        send[RIM : 2 * RIM, :] = acc[pl.ds(side.beyond, RIM), :]


def outputs(x, g, one, hopped, w_ref, bias_ref):
    bias = bias_ref[...]
    out = (
        mixed(x, both_maps(w_ref[0]))
        + mixed(one, both_maps(w_ref[1]))
        + mixed(2.0 * hopped - x, both_maps(w_ref[2]))
        + jnp.concatenate([bias, bias], axis=1)
    )
    return out, mixed(g, both_maps(w_ref[0] - w_ref[2]).T)


def own_cat(cols, cat, f_mid, f_b, f_a):
    put_cat(cat, 2 * RIM, f_mid[...])
    for side, first in zip(both_sides(cols), (f_b, f_a)):
        put_cat(cat, side.slots, first[...])


def last_mid_kernel(
    cols, fa_ref, x_ref, g_ref, f_mid, f_b, f_a, u2_ref, w_ref, bias_ref,
    out_hbm, back_hbm, cat, second, out_ref, back_ref, sem,
):
    own_cat(cols, cat, f_mid, f_b, f_a)
    hop(cols, fa_ref, cat, second, mid_block)
    mid = slice(RIM, ROWS - RIM)
    out, back = outputs(x_ref[mid, :], g_ref[mid, :], f_mid[...], second[...], w_ref, bias_ref)
    out_ref[...] = out
    back_ref[...] = back + u2_ref[mid, :]
    copies = [
        pltpu.make_async_copy(value, to.at[pl.ds(RIM, MID * PB)], sem.at[n])
        for n, (value, to) in enumerate(((out_ref, out_hbm), (back_ref, back_hbm)))
    ]
    for copy in copies:
        copy.start()
    for copy in copies:
        copy.wait()


def last_rim_kernel(
    cols, fa_b, fa_a, x_ref, g_ref, f_mid, f_b, f_a, r_b, r_a, u2_ref, w_ref, bias_ref, o_in, b_in,
    out_hbm, back_hbm, cat, second, out_ref, back_ref, sem,
):
    del o_in, b_in
    sides = both_sides(cols)
    own_cat(cols, cat, f_mid, f_b, f_a)
    for side, r in zip(sides, (r_b, r_a)):
        put_cat(cat, side.beyond, r[0:RIM, :])
    for n, (side, fa_ref) in enumerate(zip(sides, (fa_b, fa_a))):
        hop(cols, fa_ref, cat, second, side.block, HB, n * RIM)
    first = jnp.concatenate([f_b[...], f_a[...]], axis=0)
    out, back = outputs(
        side_rows(x_ref, sides), side_rows(g_ref, sides), first, second[...], w_ref, bias_ref
    )
    back = back + side_rows(u2_ref, sides)
    for n, (side, r) in enumerate(zip(sides, (r_b, r_a))):
        half = pl.ds(side.half, RIM)
        out_ref[half, :] = out[n * RIM : (n + 1) * RIM]
        back_ref[half, :] = back[n * RIM : (n + 1) * RIM] + r[RIM : 2 * RIM, :]
    copies = [
        pltpu.make_async_copy(
            value.at[pl.ds(n * RIM, RIM)], to.at[pl.ds(n * (ROWS - RIM), RIM)], sem.at[2 * k + n]
        )
        for k, (value, to) in enumerate(((out_ref, out_hbm), (back_ref, back_hbm)))
        for n in range(2)
    ]
    for copy in copies:
        copy.start()
    for copy in copies:
        copy.wait()


def pairs_kernel(cols, own, near, following, far, total_ref):
    place = cols[0:1, 0:1] // BLK_DEV
    z = jnp.bitwise_and(place // 8, 7)
    q, step = z // 2, 2 * jnp.bitwise_and(z, 1) - 1
    at = [jnp.bitwise_and(q + offset, 3) for offset in (0, step, -step)]
    terms = []
    for k in range(4):
        term = far[...]
        for source, value in zip(at, (own, near, following)):
            term = jnp.where(jnp.broadcast_to(source, term.shape) == k, value[...], term)
        terms.append(term)
    total_ref[...] = (terms[0] + terms[1]) + (terms[2] + terms[3])


def final_kernel(cols, mine, theirs, weight_ref, bias_ref):
    core = jnp.bitwise_and(cols[0:1, 0:1] // BLK_DEV, 1)
    first = jnp.broadcast_to(core, mine.shape) == 0
    top = jnp.where(first, mine[...], theirs[...])
    bottom = jnp.where(first, theirs[...], mine[...])
    rest = C - HALF
    for k, (upper, lower) in enumerate(
        ((top, bottom), (pltpu.roll(top, C, 1), pltpu.roll(bottom, C, 1)))
    ):
        weight_ref[k, 0:HALF, :] = upper[:HALF, :C]
        weight_ref[k, HALF:C, :] = lower[:rest, :C]
        weight_ref[2, k * (C // 2) : (k + 1) * (C // 2), :] = lower[rest:HALF, :C]
    bias_ref[...] = top[HALF : HALF + 1, :C]


def call(kernel, out, specs, scratch, flops, moved, places=None, aliases=None):
    return pl.pallas_call(
        kernel,
        out_shape=[jax.ShapeDtypeStruct(s, d) for s, d in out],
        in_specs=specs,
        out_specs=places or [VMEM] * len(out),
        input_output_aliases=aliases or {},
        scratch_shapes=scratch,
        compiler_params=pltpu.CompilerParams(vmem_limit_bytes=24 * 1024 * 1024),
        cost_estimate=pl.CostEstimate(flops=flops, bytes_accessed=moved, transcendentals=0),
    )


def index(a, b, c, s):
    return ((a * SHAPE[1] + b) * SHAPE[2] + c) * SHAPE[3] + s


def place(i):
    return (i // 64, (i // 8) % 8, (i // 2) % 4, i % 2)


COUNT = 256
IN_CHIP = [(i, i ^ 1) for i in range(COUNT)]
CROSS = [(i, (i + 1) % COUNT) if i % 2 else (i, (i - 1) % COUNT) for i in range(COUNT)]
RING4 = ((1, 0, 3, 2), (3, 2, 1, 0))
PAIRS = (1, 0, 3, 2, 5, 4, 7, 6)
FAR = (5, 4, 7, 6, 1, 0, 3, 2)
NEXT = (6, 3, 0, 5, 2, 7, 4, 1)
NEAR = (7, 2, 1, 4, 3, 6, 5, 0)


def along(axis, table):
    pairs = []
    for i in range(COUNT):
        at = list(place(i))
        at[axis] = table[at[axis]]
        pairs.append((i, index(*at)))
    return pairs


def sent(value, pairs):
    return lax.ppermute(value, AXES, pairs)


def shards(features, lap_tiles, columns, weights, bias_term, cotangent):
    scale = 1.0 / math.sqrt(BATCH * PB * BLOCKS)
    field = ((ROWS, W2), F32)
    half = ((ROWS // 2, W2), F32)
    extended = ((EXT * PB, W2), F32)
    sums = ((2 * HALF + 8, W2), F32)
    share = ((HALF + 8, W2), F32)
    natural = ((MID, 2 * PB, NB * PB), BF16)
    turned = ((MID, NB * PB, 2 * PB), BF16)
    raw = ((NB, BLK_DEV // 8, CHUNKS * 8, 128), F32)
    cat = pltpu.VMEM((EXT * PB, 2 * W2), BF16)
    half_scratch = pltpu.VMEM((ROWS // 2, W2), F32)

    def scaled(kernel):
        def body(*refs):
            kernel(*refs, scale=scale)

        return body

    in_hbm = [
        pltpu.with_memory_space_constraint(value, pltpu.HBM)
        for value in (columns.T, jnp.transpose(lap_tiles, (1, 0, 2)), cotangent, features)
    ]
    quarter = ((RIM, W2), F32)
    natural_4 = ((HB, 2 * PB, NB * PB), BF16)
    turned_4 = ((HB, NB * PB, 2 * PB), BF16)
    cols, raw, fa_b, at_b, acc, s_b = call(
        far_kernel,
        [((NB, BLK_DEV), jnp.int32), raw, natural_4, turned_4, extended, half],
        [HBM] * 4,
        [
            pltpu.SMEM((NB, BLK_DEV), jnp.int32), pltpu.VMEM(*quarter),
            pltpu.SemaphoreType.DMA((2 * CHUNKS,)), pltpu.SemaphoreType.DMA((4,)),
        ],
        200_000_000, 3_000_000,
    )(*in_hbm)
    r_b = sent(s_b, CROSS)
    fa_a, at_a, acc, s_a = call(
        near_kernel, [natural_4, turned_4, extended, half], [SMEM] + [VMEM] * 4, [],
        200_000_000, 3_000_000, aliases={4: 2},
    )(cols, raw, cotangent, features, acc)
    r_a = sent(s_a, IN_CHIP)
    catted = ((EXT * PB, 2 * W2), BF16)
    fa_mid, at_mid, f_mid, u_mid, u_b, u_a, part, own_x = call(
        scaled(mid_kernel), [natural, turned, half, half, quarter, quarter, sums, catted],
        [SMEM] + [VMEM] * 4, [pltpu.VMEM(*extended)], 1_600_000_000, 9_000_000,
    )(cols, raw, cotangent, features, acc)
    f_b, f_a, u_b, u_a, keep, give, _ = call(
        scaled(meet_kernel), [quarter] * 4 + [share, share, catted],
        [SMEM] + [VMEM] * 9, [], 400_000_000, 3_000_000, aliases={3: 6},
    )(cols, fa_b, fa_a, own_x, r_b, r_a, cotangent, u_b, u_a, part)
    grads = keep + sent(give, IN_CHIP)
    (acc,) = call(
        inner_mid_kernel, [extended], [SMEM] + [VMEM] * 4, [half_scratch],
        400_000_000, 3_000_000,
    )(cols, at_mid, cotangent, u_mid, weights)
    u2, s_b, s_a, _ = call(
        inner_rim_kernel, [field, half, half, extended], [SMEM] + [VMEM] * 9,
        [half_scratch], 400_000_000, 3_000_000, aliases={9: 3},
    )(cols, at_b, at_a, cotangent, u_b, u_a, weights, f_b, f_a, acc)
    s_b = sent(s_b, CROSS)
    s_a = sent(s_a, IN_CHIP)
    bias_row = bias_term.reshape(1, C)
    scratch = [cat, half_scratch, half_scratch, half_scratch]
    output, input_grad = call(
        last_mid_kernel, [field, field], [SMEM] + [VMEM] * 9,
        scratch + [pltpu.SemaphoreType.DMA((2,))], 600_000_000, 4_000_000, places=[HBM, HBM],
    )(cols, fa_mid, features, cotangent, f_mid, f_b, f_a, u2, weights, bias_row)
    output, input_grad = call(
        last_rim_kernel, [field, field], [SMEM] + [VMEM] * 12 + [HBM, HBM],
        scratch + [pltpu.SemaphoreType.DMA((4,))], 600_000_000, 5_000_000,
        places=[HBM, HBM], aliases={13: 0, 14: 1},
    )(
        cols, fa_b, fa_a, features, cotangent, f_mid, f_b, f_a, s_b, s_a, u2, weights, bias_row,
        output, input_grad,
    )
    grads = grads + sent(grads, along(2, RING4[0]))
    grads = grads + sent(grads, along(2, RING4[1]))
    grads = grads + sent(grads, along(0, RING4[0]))
    grads = grads + sent(grads, along(0, RING4[1]))
    grads = grads + sent(grads, along(1, PAIRS))
    far = sent(grads, along(1, FAR))
    following = sent(grads, along(1, NEXT))
    near = sent(grads, along(1, NEAR))
    (grads,) = call(pairs_kernel, [share], [VMEM] * 5, [], 1000, 100_000)(
        cols, grads, near, following, far
    )
    theirs = sent(grads, IN_CHIP)
    weight_grad, bias_grad = call(
        final_kernel, [((3, C, C), F32), ((1, C), F32)], [VMEM] * 3, [],
        1000, 100_000,
    )(cols, grads, theirs)
    return output, input_grad, weight_grad, bias_grad.reshape(C)


def solution(mesh):
    grid = Mesh(mesh.devices.reshape(*SHAPE), AXES)
    placed = (P(AXES, None), P(AXES, None, None), P(AXES, None), P(), P(), P(AXES, None))

    return jax.shard_map(
        shards,
        mesh=grid,
        in_specs=placed,
        out_specs=(P(AXES, None), P(AXES, None), P(), P()),
        check_vma=False,
    )
```

```python
import math

import jax
import jax.numpy as jnp
from jax import lax
from jax.experimental import pallas as pl
from jax.experimental.pallas import tpu as pltpu
from jax.sharding import Mesh
from jax.sharding import PartitionSpec as P


C = 64
BATCH = 2
PB = 64
NB = 6
HB = 4
BLK_DEV = 16
ROWS = BLK_DEV * PB
RIM = HB * PB
EXT = BLK_DEV + 2 * HB
MID = BLK_DEV - 2 * HB
HALF = 3 * C // 4
W2 = BATCH * C
CHUNKS = PB * PB // 128
AXES = ("patch_0", "patch_1", "patch_2", "strip")
SHAPE = (4, 8, 4, 2)
BLOCKS = 4096
F32 = jnp.float32
BF16 = jnp.bfloat16
VMEM = pl.BlockSpec(memory_space=pltpu.VMEM)
SMEM = pl.BlockSpec(memory_space=pltpu.SMEM)
HBM = pl.BlockSpec(memory_space=pltpu.HBM)


def split(value):
    high = value.astype(BF16)
    return high, (value - high.astype(F32)).astype(BF16)


def mm(a, b):
    return jnp.dot(a, b, preferred_element_type=F32)


def mm_tn(a, b):
    return lax.dot_general(a, b, (((0,), (0,)), ((), ())), preferred_element_type=F32)


def slot_of(cols, b, j):
    return jnp.bitwise_and(cols[j, b] - cols[0, 0] + HB, BLOCKS - 1)


def strip_of(cols):
    return jnp.bitwise_and(cols[0, 0] // BLK_DEV, 1)


class Side:
    def __init__(self, end):
        self.own = pl.multiple_of(end * (ROWS - RIM), RIM)
        self.slots = pl.multiple_of(self.own + RIM, RIM)
        self.beyond = pl.multiple_of(end * ((BLK_DEV + HB) * PB), RIM)
        self.half = pl.multiple_of(end * RIM, RIM)
        self.first = end * (BLK_DEV - HB)

    def block(self, i):
        return self.first + i


def both_sides(cols):
    strip = strip_of(cols)
    return Side(strip), Side(1 - strip)


def mid_block(i):
    return i + HB


def block_rows(ref, at):
    return jnp.concatenate(
        [ref[pl.ds(at, PB // 2, stride=2), :], ref[pl.ds(at + 1, PB // 2, stride=2), :]], axis=0
    )


def rows_of(slot):
    return pl.ds(pl.multiple_of(slot * PB, PB), PB)


def spread(cols, at_ref, vec_ref, acc, block, count=MID, start=0):
    def one(i, carry):
        b = block(i)
        high, low = split(block_rows(vec_ref, start + i * PB))
        rhs = jnp.concatenate([high, high, low, low], axis=0)
        at = at_ref[i]
        out = mm(jnp.concatenate([at, at], axis=1), rhs)
        for j in range(NB):
            rows = rows_of(slot_of(cols, b, j))
            acc[rows, :] = acc[rows, :] + out[j * PB : (j + 1) * PB]
        return carry

    lax.fori_loop(0, count, one, 0, unroll=count)


def hop(cols, fa_ref, cat, out_ref, block, count=MID, start=0):
    def one(i, carry):
        b = block(i)
        rhs = jnp.concatenate([cat[rows_of(slot_of(cols, b, j)), :] for j in range(NB)], axis=0)
        out = mm(fa_ref[i], rhs)
        out = out[:, :W2] + out[:, W2:]
        out = out[:PB] + out[PB:]
        out_ref[pl.ds(start + i * PB, PB // 2, stride=2), :] = out[: PB // 2]
        out_ref[pl.ds(start + i * PB + 1, PB // 2, stride=2), :] = out[PB // 2 :]
        return carry

    lax.fori_loop(0, count, one, 0, unroll=count)


def put_cat(cat, start, value):
    high, low = split(value)
    cat[pl.ds(start, value.shape[0]), :] = jnp.concatenate([high, low], axis=1)


def build(raw, fa_ref, at_ref, block, count=MID):
    low_lanes = lax.broadcasted_iota(jnp.int32, (CHUNKS, 128), 1) < PB

    def one(i, carry):
        b = block(i)
        group, rows = b // 8, pl.ds(b % 8, CHUNKS, stride=8)
        for pair in range(NB // 2):
            even = raw[2 * pair, group, rows, :]
            odd = raw[2 * pair + 1, group, rows, :]
            top = jnp.where(low_lanes, even, pltpu.roll(odd, PB, 1))
            bottom = jnp.where(low_lanes, pltpu.roll(even, PB, 1), odd)
            both = jnp.concatenate([top, bottom], axis=0)
            high = both.astype(BF16)
            low = (both - high.astype(F32)).astype(BF16)
            lanes = pl.ds(pair * 128, 128)
            stacked = jnp.concatenate([high, low], axis=0)
            fa_ref[i, :, lanes] = stacked
            at_ref[i, lanes, :] = stacked.T
        return carry

    lax.fori_loop(0, count, one, 0, unroll=count)


def far_kernel(
    cols_hbm, tiles, g_hbm, x_hbm,
    cols_ref, raw, fa_ref, at_ref, acc, send,
    cols, g_rim, sem, small,
):
    strip = lax.axis_index("strip")
    side = Side(strip)

    def group_copies(group, n):
        return [
            pltpu.make_async_copy(
                tiles.at[:, pl.ds(pl.multiple_of(8 * group, 8), 8), pl.ds(k * 128, 128)],
                raw.at[:, group, pl.ds(8 * k, 8), :],
                sem.at[n * CHUNKS + k],
            )
            for k in range(CHUNKS)
        ]

    now, later = group_copies(strip, 0), group_copies(1 - strip, 1)
    rows = pl.ds(side.own, RIM)
    soon = [
        pltpu.make_async_copy(cols_hbm, cols, small.at[0]),
        pltpu.make_async_copy(g_hbm.at[rows], g_rim, small.at[1]),
    ]
    late = [
        pltpu.make_async_copy(cols_hbm, cols_ref, small.at[2]),
        pltpu.make_async_copy(x_hbm.at[rows], send.at[pl.ds(0, RIM)], small.at[3]),
    ]
    for copy in now + soon + late + later:
        copy.start()
    acc[...] = jnp.zeros_like(acc)
    for copy in now:
        copy.wait()
    build(raw, fa_ref, at_ref, side.block, HB)
    for copy in soon:
        copy.wait()
    spread(cols, at_ref, g_rim, acc, side.block, HB)
    send[RIM : 2 * RIM, :] = acc[pl.ds(side.beyond, RIM), :]
    for copy in late + later:
        copy.wait()


def near_kernel(cols, raw, g_ref, x_ref, acc_in, fa_ref, at_ref, acc, send):
    del acc_in
    _, side = both_sides(cols)
    build(raw, fa_ref, at_ref, side.block, HB)
    spread(cols, at_ref, g_ref, acc, side.block, HB, side.own)
    send[0:RIM, :] = x_ref[pl.ds(side.own, RIM), :]
    send[RIM : 2 * RIM, :] = acc[pl.ds(side.beyond, RIM), :]


def maps_sum(full):
    return full[:C] + pltpu.roll(full[C:], C, 1)


def products(left, right):
    a = jnp.concatenate([h for value in left for h in split(value)], axis=1)
    b = jnp.concatenate([h for value in right for h in split(value)], axis=1)
    out = mm_tn(a, b)
    result = []
    for p in range(len(left)):
        band = out[2 * p * W2 : (2 * p + 1) * W2] + out[(2 * p + 1) * W2 : (2 * p + 2) * W2]
        result.append(
            [
                band[:, 2 * q * W2 : (2 * q + 1) * W2] + band[:, (2 * q + 1) * W2 : (2 * q + 2) * W2]
                for q in range(len(right))
            ]
        )
    return result


def packed(zero, one, two):
    low_lanes = lax.broadcasted_iota(jnp.int32, (C, 128), 1) < C
    two = maps_sum(two)
    one = pltpu.roll(maps_sum(one), C, 1)
    if zero is None:
        top = jnp.where(low_lanes, 0.0, one)
    else:
        top = jnp.where(low_lanes, maps_sum(zero), one)
    bottom = jnp.where(low_lanes[: C // 2], two[: C // 2], pltpu.roll(two[C // 2 :], C, 1))
    return jnp.concatenate([top, bottom], axis=0)


def both_maps(weight):
    zero = jnp.zeros_like(weight)
    return jnp.concatenate(
        [jnp.concatenate([weight, zero], axis=1), jnp.concatenate([zero, weight], axis=1)], axis=0
    )


def mixed(value, weight):
    high, low = split(value)
    w_high, w_low = split(weight)
    row = jnp.concatenate([w_high, w_low], axis=1)
    out = mm(jnp.concatenate([high, low], axis=1), jnp.concatenate([row, row], axis=0))
    return out[:, :W2] + out[:, W2:]


def mid_kernel(
    cols, raw, g_ref, x_ref, acc_in,
    fa_ref, at_ref, first_ref, u_mid, u_b, u_a, part_ref, cat,
    acc, *, scale,
):
    put_cat(cat, RIM, x_ref[...])
    acc[...] = acc_in[...]
    build(raw, fa_ref, at_ref, mid_block)
    g_mid = g_ref.at[pl.ds(RIM, MID * PB)]
    spread(cols, at_ref, g_mid, acc, mid_block)
    u_mid[...] = acc[2 * RIM : 4 * RIM, :]
    for side, u in zip(both_sides(cols), (u_b, u_a)):
        u[...] = acc[pl.ds(side.slots, RIM), :]
    hop(cols, fa_ref, cat, first_ref, mid_block)
    ((zero,),) = products([x_ref[...]], [g_ref[...]])
    ((one, two),) = products([first_ref[...]], [g_mid[...], u_mid[...]])
    part_ref[0 : C + C // 2, :] = scale * packed(zero, one, 2.0 * two - zero)
    bias = scale * jnp.sum(g_ref[...], axis=0, keepdims=True)
    part_ref[C + C // 2 :, :] = jnp.broadcast_to(bias + pltpu.roll(bias, C, 1), (8, 128))


def side_rows(ref, sides):
    return jnp.concatenate([ref[pl.ds(side.own, RIM), :] for side in sides], axis=0)


def meet_kernel(
    cols, fa_b, fa_a, cat_in, r_b, r_a, g_ref, p_b, p_a, part_ref,
    f_b, f_a, u_b, u_a, keep_ref, give_ref, cat, *, scale
):
    del cat_in
    sides = both_sides(cols)
    for side, r, p, u in zip(sides, (r_b, r_a), (p_b, p_a), (u_b, u_a)):
        put_cat(cat, side.beyond, r[0:RIM, :])
        u[...] = p[...] + r[RIM : 2 * RIM, :]
    for side, fa_ref, first in zip(sides, (fa_b, fa_a), (f_b, f_a)):
        hop(cols, fa_ref, cat, first, side.block, HB)
    first = jnp.concatenate([f_b[...], f_a[...]], axis=0)
    u = jnp.concatenate([u_b[...], u_a[...]], axis=0)
    ((one, two),) = products([first], [side_rows(g_ref, sides), u])
    total = part_ref[0 : 2 * HALF, :] + scale * packed(None, one, 2.0 * two)
    lower = strip_of(cols) == 0
    keep_ref[0:HALF, :] = jnp.where(lower, total[:HALF], total[HALF:])
    give_ref[0:HALF, :] = jnp.where(lower, total[HALF:], total[:HALF])
    keep_ref[HALF:, :] = part_ref[2 * HALF :, :]
    give_ref[HALF:, :] = part_ref[2 * HALF :, :]


def inner_rows(g, u, w_ref):
    return mixed(g, both_maps(w_ref[1]).T) + 2.0 * mixed(u, both_maps(w_ref[2]).T)


def inner_mid_kernel(cols, at_ref, g_ref, u_ref, w_ref, acc, inner):
    inner[...] = inner_rows(g_ref[RIM : ROWS - RIM, :], u_ref[...], w_ref)
    acc[...] = jnp.zeros_like(acc)
    spread(cols, at_ref, inner, acc, mid_block)


def inner_rim_kernel(
    cols, at_b, at_a, g_ref, u_b, u_a, w_ref, f_b, f_a, acc_in,
    u2_ref, send_b, send_a, acc, inner,
):
    del acc_in
    sides = both_sides(cols)
    u = jnp.concatenate([u_b[...], u_a[...]], axis=0)
    inner[...] = inner_rows(side_rows(g_ref, sides), u, w_ref)
    for n, (side, at_ref) in enumerate(zip(sides, (at_b, at_a))):
        spread(cols, at_ref, inner, acc, side.block, HB, n * RIM)
    u2_ref[...] = acc[RIM : RIM + ROWS, :]
    for side, first, send in zip(sides, (f_b, f_a), (send_b, send_a)):
        send[0:RIM, :] = first[...]
        send[RIM : 2 * RIM, :] = acc[pl.ds(side.beyond, RIM), :]


def outputs(x, g, one, hopped, w_ref, bias_ref):
    bias = bias_ref[...]
    out = (
        mixed(x, both_maps(w_ref[0]))
        + mixed(one, both_maps(w_ref[1]))
        + mixed(2.0 * hopped - x, both_maps(w_ref[2]))
        + jnp.concatenate([bias, bias], axis=1)
    )
    return out, mixed(g, both_maps(w_ref[0] - w_ref[2]).T)


def own_cat(cols, cat, f_mid, f_b, f_a):
    put_cat(cat, 2 * RIM, f_mid[...])
    for side, first in zip(both_sides(cols), (f_b, f_a)):
        put_cat(cat, side.slots, first[...])


def last_mid_kernel(
    cols, fa_ref, x_ref, g_ref, f_mid, f_b, f_a, u2_ref, w_ref, bias_ref,
    out_hbm, back_hbm, cat, second, out_ref, back_ref, sem,
):
    own_cat(cols, cat, f_mid, f_b, f_a)
    hop(cols, fa_ref, cat, second, mid_block)
    mid = slice(RIM, ROWS - RIM)
    out, back = outputs(x_ref[mid, :], g_ref[mid, :], f_mid[...], second[...], w_ref, bias_ref)
    out_ref[...] = out
    back_ref[...] = back + u2_ref[mid, :]
    copies = [
        pltpu.make_async_copy(value, to.at[pl.ds(RIM, MID * PB)], sem.at[n])
        for n, (value, to) in enumerate(((out_ref, out_hbm), (back_ref, back_hbm)))
    ]
    for copy in copies:
        copy.start()
    for copy in copies:
        copy.wait()


def last_rim_kernel(
    cols, fa_b, fa_a, x_ref, g_ref, f_mid, f_b, f_a, r_b, r_a, u2_ref, w_ref, bias_ref, o_in, b_in,
    out_hbm, back_hbm, cat, second, out_ref, back_ref, sem,
):
    del o_in, b_in
    sides = both_sides(cols)
    own_cat(cols, cat, f_mid, f_b, f_a)
    for side, r in zip(sides, (r_b, r_a)):
        put_cat(cat, side.beyond, r[0:RIM, :])
    for n, (side, fa_ref) in enumerate(zip(sides, (fa_b, fa_a))):
        hop(cols, fa_ref, cat, second, side.block, HB, n * RIM)
    first = jnp.concatenate([f_b[...], f_a[...]], axis=0)
    out, back = outputs(
        side_rows(x_ref, sides), side_rows(g_ref, sides), first, second[...], w_ref, bias_ref
    )
    back = back + side_rows(u2_ref, sides)
    for n, (side, r) in enumerate(zip(sides, (r_b, r_a))):
        half = pl.ds(side.half, RIM)
        out_ref[half, :] = out[n * RIM : (n + 1) * RIM]
        back_ref[half, :] = back[n * RIM : (n + 1) * RIM] + r[RIM : 2 * RIM, :]
    copies = [
        pltpu.make_async_copy(
            value.at[pl.ds(n * RIM, RIM)], to.at[pl.ds(n * (ROWS - RIM), RIM)], sem.at[2 * k + n]
        )
        for k, (value, to) in enumerate(((out_ref, out_hbm), (back_ref, back_hbm)))
        for n in range(2)
    ]
    for copy in copies:
        copy.start()
    for copy in copies:
        copy.wait()


def pairs_kernel(cols, own, near, following, far, total_ref):
    place = cols[0:1, 0:1] // BLK_DEV
    z = jnp.bitwise_and(place // 8, 7)
    q, step = z // 2, 2 * jnp.bitwise_and(z, 1) - 1
    at = [jnp.bitwise_and(q + offset, 3) for offset in (0, step, -step)]
    terms = []
    for k in range(4):
        term = far[...]
        for source, value in zip(at, (own, near, following)):
            term = jnp.where(jnp.broadcast_to(source, term.shape) == k, value[...], term)
        terms.append(term)
    total_ref[...] = (terms[0] + terms[1]) + (terms[2] + terms[3])


def final_kernel(cols, mine, theirs, weight_ref, bias_ref):
    core = jnp.bitwise_and(cols[0:1, 0:1] // BLK_DEV, 1)
    first = jnp.broadcast_to(core, mine.shape) == 0
    top = jnp.where(first, mine[...], theirs[...])
    bottom = jnp.where(first, theirs[...], mine[...])
    rest = C - HALF
    for k, (upper, lower) in enumerate(
        ((top, bottom), (pltpu.roll(top, C, 1), pltpu.roll(bottom, C, 1)))
    ):
        weight_ref[k, 0:HALF, :] = upper[:HALF, :C]
        weight_ref[k, HALF:C, :] = lower[:rest, :C]
        weight_ref[2, k * (C // 2) : (k + 1) * (C // 2), :] = lower[rest:HALF, :C]
    bias_ref[...] = top[HALF : HALF + 1, :C]


def call(kernel, out, specs, scratch, flops, moved, places=None, aliases=None):
    return pl.pallas_call(
        kernel,
        out_shape=[jax.ShapeDtypeStruct(s, d) for s, d in out],
        in_specs=specs,
        out_specs=places or [VMEM] * len(out),
        input_output_aliases=aliases or {},
        scratch_shapes=scratch,
        compiler_params=pltpu.CompilerParams(vmem_limit_bytes=24 * 1024 * 1024),
        cost_estimate=pl.CostEstimate(flops=flops, bytes_accessed=moved, transcendentals=0),
    )


def index(a, b, c, s):
    return ((a * SHAPE[1] + b) * SHAPE[2] + c) * SHAPE[3] + s


def place(i):
    return (i // 64, (i // 8) % 8, (i // 2) % 4, i % 2)


COUNT = 256
IN_CHIP = [(i, i ^ 1) for i in range(COUNT)]
CROSS = [(i, (i + 1) % COUNT) if i % 2 else (i, (i - 1) % COUNT) for i in range(COUNT)]
RING4 = ((1, 0, 3, 2), (3, 2, 1, 0))
PAIRS = (1, 0, 3, 2, 5, 4, 7, 6)
FAR = (5, 4, 7, 6, 1, 0, 3, 2)
NEXT = (6, 3, 0, 5, 2, 7, 4, 1)
NEAR = (7, 2, 1, 4, 3, 6, 5, 0)


def along(axis, table):
    pairs = []
    for i in range(COUNT):
        at = list(place(i))
        at[axis] = table[at[axis]]
        pairs.append((i, index(*at)))
    return pairs


def sent(value, pairs):
    return lax.ppermute(value, AXES, pairs)


def shards(features, lap_tiles, columns, weights, bias_term, cotangent):
    scale = 1.0 / math.sqrt(BATCH * PB * BLOCKS)
    field = ((ROWS, W2), F32)
    half = ((ROWS // 2, W2), F32)
    extended = ((EXT * PB, W2), F32)
    sums = ((2 * HALF + 8, W2), F32)
    share = ((HALF + 8, W2), F32)
    natural = ((MID, 2 * PB, NB * PB), BF16)
    turned = ((MID, NB * PB, 2 * PB), BF16)
    raw = ((NB, BLK_DEV // 8, CHUNKS * 8, 128), F32)
    cat = pltpu.VMEM((EXT * PB, 2 * W2), BF16)
    half_scratch = pltpu.VMEM((ROWS // 2, W2), F32)

    def scaled(kernel):
        def body(*refs):
            kernel(*refs, scale=scale)

        return body

    in_hbm = [
        pltpu.with_memory_space_constraint(value, pltpu.HBM)
        for value in (columns.T, jnp.transpose(lap_tiles, (1, 0, 2)), cotangent, features)
    ]
    quarter = ((RIM, W2), F32)
    natural_4 = ((HB, 2 * PB, NB * PB), BF16)
    turned_4 = ((HB, NB * PB, 2 * PB), BF16)
    cols, raw, fa_b, at_b, acc, s_b = call(
        far_kernel,
        [((NB, BLK_DEV), jnp.int32), raw, natural_4, turned_4, extended, half],
        [HBM] * 4,
        [
            pltpu.SMEM((NB, BLK_DEV), jnp.int32), pltpu.VMEM(*quarter),
            pltpu.SemaphoreType.DMA((2 * CHUNKS,)), pltpu.SemaphoreType.DMA((4,)),
        ],
        200_000_000, 3_000_000,
    )(*in_hbm)
    r_b = sent(s_b, CROSS)
    fa_a, at_a, acc, s_a = call(
        near_kernel, [natural_4, turned_4, extended, half], [SMEM] + [VMEM] * 4, [],
        200_000_000, 3_000_000, aliases={4: 2},
    )(cols, raw, cotangent, features, acc)
    r_a = sent(s_a, IN_CHIP)
    catted = ((EXT * PB, 2 * W2), BF16)
    fa_mid, at_mid, f_mid, u_mid, u_b, u_a, part, own_x = call(
        scaled(mid_kernel), [natural, turned, half, half, quarter, quarter, sums, catted],
        [SMEM] + [VMEM] * 4, [pltpu.VMEM(*extended)], 1_600_000_000, 9_000_000,
    )(cols, raw, cotangent, features, acc)
    f_b, f_a, u_b, u_a, keep, give, _ = call(
        scaled(meet_kernel), [quarter] * 4 + [share, share, catted],
        [SMEM] + [VMEM] * 9, [], 400_000_000, 3_000_000, aliases={3: 6},
    )(cols, fa_b, fa_a, own_x, r_b, r_a, cotangent, u_b, u_a, part)
    grads = keep + sent(give, IN_CHIP)
    (acc,) = call(
        inner_mid_kernel, [extended], [SMEM] + [VMEM] * 4, [half_scratch],
        400_000_000, 3_000_000,
    )(cols, at_mid, cotangent, u_mid, weights)
    u2, s_b, s_a, _ = call(
        inner_rim_kernel, [field, half, half, extended], [SMEM] + [VMEM] * 9,
        [half_scratch], 400_000_000, 3_000_000, aliases={9: 3},
    )(cols, at_b, at_a, cotangent, u_b, u_a, weights, f_b, f_a, acc)
    s_b = sent(s_b, CROSS)
    s_a = sent(s_a, IN_CHIP)
    bias_row = bias_term.reshape(1, C)
    scratch = [cat, half_scratch, half_scratch, half_scratch]
    output, input_grad = call(
        last_mid_kernel, [field, field], [SMEM] + [VMEM] * 9,
        scratch + [pltpu.SemaphoreType.DMA((2,))], 600_000_000, 4_000_000, places=[HBM, HBM],
    )(cols, fa_mid, features, cotangent, f_mid, f_b, f_a, u2, weights, bias_row)
    output, input_grad = call(
        last_rim_kernel, [field, field], [SMEM] + [VMEM] * 12 + [HBM, HBM],
        scratch + [pltpu.SemaphoreType.DMA((4,))], 600_000_000, 5_000_000,
        places=[HBM, HBM], aliases={13: 0, 14: 1},
    )(
        cols, fa_b, fa_a, features, cotangent, f_mid, f_b, f_a, s_b, s_a, u2, weights, bias_row,
        output, input_grad,
    )
    opposite = sent(grads, along(2, (2, 3, 0, 1)))
    beside = sent(grads, along(2, RING4[0]))
    other = sent(grads, along(2, RING4[1]))
    grads = (grads + beside) + (other + opposite)
    opposite = sent(grads, along(0, (2, 3, 0, 1)))
    beside = sent(grads, along(0, RING4[0]))
    other = sent(grads, along(0, RING4[1]))
    grads = (grads + beside) + (other + opposite)
    grads = grads + sent(grads, along(1, PAIRS))
    far = sent(grads, along(1, FAR))
    following = sent(grads, along(1, NEXT))
    near = sent(grads, along(1, NEAR))
    (grads,) = call(pairs_kernel, [share], [VMEM] * 5, [], 1000, 100_000)(
        cols, grads, near, following, far
    )
    theirs = sent(grads, IN_CHIP)
    weight_grad, bias_grad = call(
        final_kernel, [((3, C, C), F32), ((1, C), F32)], [VMEM] * 3, [],
        1000, 100_000,
    )(cols, grads, theirs)
    return output, input_grad, weight_grad, bias_grad.reshape(C)


def solution(mesh):
    grid = Mesh(mesh.devices.reshape(*SHAPE), AXES)
    placed = (P(AXES, None), P(AXES, None, None), P(AXES, None), P(), P(), P(AXES, None))

    return jax.shard_map(
        shards,
        mesh=grid,
        in_specs=placed,
        out_specs=(P(AXES, None), P(AXES, None), P(), P()),
        check_vma=False,
    )
```
